256 devices in a mesh: gx: 16 (over x_hi, z), gy: 16 (over y, x_lo, core).
Axes of the slice: x: 4 (x_hi: 2, x_lo: 2; x = x_hi * 2 + x_lo), y: 4, z: 8, core: 2. Of those that a mesh axis runs over, the one named last changes fastest.
Arguments:
- positions: float32 [16, 16, 3, 3, 128], P('gx', 'gy'), may hold values from 0 to 10
- velocities: float32 [16, 16, 3, 3, 128], P('gx', 'gy'), may hold values from -6 to 6
- forces: float32 [16, 16, 3, 3, 128], P('gx', 'gy'), may hold values from -6 to 6
- noise: float32 [16, 16, 3, 3, 128], P('gx', 'gy'), may hold values from -6 to 6
- species: int32 [16, 16, 3, 128], P('gx', 'gy'), may hold values from 0 to 5
- counts: int32 [16, 16, 3], P('gx', 'gy'), may hold values from 64 to 128
- pair_list: int32 [16, 16, 3, 13], P('gx', 'gy'), may hold values 0 or 1
- masses: float32 [6], replicated, may hold values from 1 to 4
- embedding: bfloat16 [6, 128], replicated, may hold values from -6 to 6
- radial_one: float32 [8, 128], replicated, may hold values from -0.625 to 0.625
- mix_one: bfloat16 [128, 128], replicated, may hold values from -0.5 to 0.5
- radial_two: bfloat16 [8, 128], replicated, may hold values from -0.75 to 0.75
- mix_two: bfloat16 [128, 128], replicated, may hold values from -0.5 to 0.5
- readout: float32 [128], replicated, may hold values from -1.5 to 1.5
Outputs:
- new_positions: float32 [16, 16, 3, 3, 128], P('gx', 'gy')
- new_velocities: float32 [16, 16, 3, 3, 128], P('gx', 'gy')
- new_forces: float32 [16, 16, 3, 3, 128], P('gx', 'gy')
The draws below stay inside these ranges and needn't reach their ends.
Inputs may be any that keep to these rules, and one draw needn't show every extreme that they name: `species` holds a species index 0 to 5 for every slot, padding slots included. The first counts[b] slots of block b hold atoms, the others are padding. `pair_list`: entry h of a block flags its pair with the neighbour block at the h-th of the 13 offsets (ox, oy, oz) with entries -1, 0, 1 that follow (0, 0, 0) in lexicographic order.
All inputs are finite; a program needn't handle non-finite values.
Results may differ from the reference program's by a relative error of at most 0.01065.
Values may be sent and summed in bfloat16 or wider, within the bound.
No kernel may reach another device: no remote copies, remote signals or barrier semaphores. Data moves between devices by JAX's collectives and lax.ppermute only.
A program may use at most 128 MiB of HBM per device.

```python
import math
import jax
import jax.numpy as jnp
from jax import lax

CHANNELS = 128
RADIAL = 8
SPECIES = 6
SLOTS = 128
COLUMN = 3
BLOCKS_X = 16
BLOCKS_Y = 16


def set_ends(drawn, own_key, low, high):
    place = [jax.random.randint(jax.random.fold_in(own_key, axis), (), 0, length) for axis, length in enumerate(drawn.shape)]
    longest = drawn.shape.index(max(drawn.shape))
    next_to = place[:longest] + [(place[longest] + 1) % drawn.shape[longest]] + place[longest + 1:]
    return drawn.at[tuple(place)].set(low).at[tuple(next_to)].set(high)


def steps_of(own_key, dims, split, low, largest):
    factor_of, own = 1.0, jax.random.fold_in(own_key, 6)
    for axis_at, parts in split:
        steps = jnp.exp(jax.random.uniform(jax.random.fold_in(own, axis_at), (parts,), jnp.float32, low / len(split), largest / len(split)))
        factor_of = factor_of * jnp.repeat(steps, dims[axis_at] // parts).reshape([-1 if axis == axis_at else 1 for axis in range(len(dims))])
    return factor_of


def gaussian(stream_key, shape, scale, reach, pieces=(), kind=jnp.bfloat16):
    entries = jax.random.normal(stream_key, shape, jnp.float32) * scale
    if len(pieces) > 0:
        entries = steps_of(stream_key, shape, pieces, -0.22, 0.18) * entries
    return jnp.clip(entries, min=-reach, max=reach).astype(kind)


def setup_inputs(seed: int = 0) -> dict:
    key_list = jax.random.split(jax.random.key(seed), 15)
    positions = jnp.clip(10.0 * jax.random.uniform(key_list[0], (BLOCKS_X, BLOCKS_Y, COLUMN, 3, SLOTS), jnp.float32) ** steps_of(key_list[0], (BLOCKS_X, BLOCKS_Y, COLUMN, 3, SLOTS), ((0, 16), (1, 16)), -0.2, 0.2), 0.0, 10.0)
    velocities = gaussian(key_list[1], (BLOCKS_X, BLOCKS_Y, COLUMN, 3, SLOTS), 1.0, 6.0, ((0, 16), (1, 16)), jnp.float32)
    forces = gaussian(key_list[2], (BLOCKS_X, BLOCKS_Y, COLUMN, 3, SLOTS), 1.0, 6.0, ((0, 16), (1, 16)), jnp.float32)
    noise = gaussian(key_list[3], (BLOCKS_X, BLOCKS_Y, COLUMN, 3, SLOTS), 1.0, 6.0, ((0, 16), (1, 16)), jnp.float32)
    species = set_ends(jax.random.randint(key_list[4], (BLOCKS_X, BLOCKS_Y, COLUMN, SLOTS), 0, SPECIES), jax.random.fold_in(key_list[4], 1), 0, SPECIES - 1).astype(jnp.int32)
    counts = set_ends(jax.random.randint(key_list[5], (BLOCKS_X, BLOCKS_Y, COLUMN), SLOTS // 2, SLOTS + 1), jax.random.fold_in(key_list[5], 1), SLOTS // 2, SLOTS).astype(jnp.int32)
    pair_list = set_ends((jax.random.randint(key_list[6], (BLOCKS_X, BLOCKS_Y, COLUMN, 13), 0, 4) < 3).astype(jnp.int32), jax.random.fold_in(key_list[6], 1), 0, 1)
    masses = jnp.clip(jnp.exp(jax.random.uniform(key_list[7], (SPECIES,), jnp.float32, math.log(1.0), math.log(4.0))), 1.0, 4.0)
    embedding = gaussian(key_list[8], (SPECIES, CHANNELS), 1.0, 6.0)
    radial_one = gaussian(key_list[9], (RADIAL, CHANNELS), (2 * RADIAL * SPECIES) ** -0.5, 0.625, (), jnp.float32)
    mix_one = gaussian(key_list[10], (CHANNELS, CHANNELS), CHANNELS ** -0.5, 0.5)
    radial_two = gaussian(key_list[11], (RADIAL, CHANNELS), (8 * RADIAL) ** -0.5, 0.75)
    mix_two = gaussian(key_list[12], (CHANNELS, CHANNELS), CHANNELS ** -0.5, 0.5)
    readout = gaussian(key_list[13], (CHANNELS,), 0.25, 1.5, (), jnp.float32)
    return {"positions": positions, "velocities": velocities, "forces": forces, "noise": noise, "species": species, "counts": counts, "pair_list": pair_list, "masses": masses, "embedding": embedding, "radial_one": radial_one, "mix_one": mix_one, "radial_two": radial_two, "mix_two": mix_two, "readout": readout}


SIDE = 10.0
REACH = 5.0
HALF_STEP = 0.25
DECAY = math.exp(-0.5)

def product(form, left_side, right_side):
    return jnp.einsum(form, left_side.astype(jnp.float32), right_side.astype(jnp.float32), precision=lax.Precision.HIGHEST)

def offsets(stencil):
    return (stencil // 9 - 1, stencil // 3 % 3 - 1, stencil % 3 - 1)

def shifted(field, stencil):
    step_x, step_y, step_z = offsets(stencil)
    field = jnp.roll(field, -step_x, axis=0)
    field = jnp.roll(field, -step_y, axis=1)
    return jnp.roll(field, -step_z, axis=2)

def pair_frame(stencil, own_pos, near_pos, own_count, near_count, own_list, near_list):
    step_x, step_y, step_z = offsets(stencil)
    displacement = jnp.stack([step_x, step_y, step_z]).astype(jnp.float32) * SIDE
    separation = near_pos[..., :, None, :] + displacement[:, None, None] - own_pos[..., :, :, None]
    scaled = jnp.minimum(lax.optimization_barrier(jnp.sum(separation * separation, axis=-3)) / (REACH * REACH), 1.0)
    slot_ids = jnp.arange(own_pos.shape[-1], dtype=jnp.int32)
    own_live = (slot_ids < own_count[..., None]).astype(jnp.float32)
    near_live = (slot_ids < near_count[..., None]).astype(jnp.float32)
    ahead = jnp.take(own_list, jnp.clip(stencil - 14, 0, 12), axis=-1)
    behind = jnp.take(near_list, jnp.clip(12 - stencil, 0, 12), axis=-1)
    listed = jnp.where(stencil == 13, 1, jnp.where(stencil > 13, ahead, behind)).astype(jnp.float32)
    diagonal_pair = jnp.logical_and(stencil == 13, slot_ids[:, None] == slot_ids[None, :])
    weight = listed[..., None, None] * own_live[..., :, None] * near_live[..., None, :]
    weight = weight * jnp.where(diagonal_pair, 0.0, 1.0).astype(jnp.float32)
    return (separation, scaled, weight)

def radial_terms(scaled, weight, orders):
    wavenumbers = math.pi * jnp.arange(orders, dtype=jnp.int32).astype(jnp.float32)[:, None, None]
    angles = wavenumbers * scaled[..., None, :, :]
    leftover = (1.0 - scaled)[..., None, :, :]
    return weight[..., None, :, :] * leftover * leftover * jnp.cos(angles)

def radial_slope(scaled, weight, orders):
    wavenumbers = math.pi * jnp.arange(orders, dtype=jnp.int32).astype(jnp.float32)[:, None, None]
    angles = wavenumbers * scaled[..., None, :, :]
    leftover = (1.0 - scaled)[..., None, :, :]
    return weight[..., None, :, :] * (-2.0 * leftover * jnp.cos(angles) - wavenumbers * leftover * leftover * jnp.sin(angles))

def silu_slope(values):
    sigmoid = jax.nn.sigmoid(values)
    return sigmoid * (1.0 + values * (1.0 - sigmoid))

def force_field(positions, species, counts, pair_list, embedding, radial_one, mix_one, radial_two, mix_two, readout):
    species_total = embedding.shape[0]
    orders = radial_one.shape[0]
    slot_total = positions.shape[-1]
    own_kinds = (species[..., None] == jnp.arange(species_total, dtype=jnp.int32)).astype(jnp.bfloat16)
    slot_ids = jnp.arange(slot_total, dtype=jnp.int32)
    own_live = (slot_ids < counts[..., None]).astype(jnp.float32)
    base_features = product('xyzas,sc->xyzac', own_kinds, embedding).astype(jnp.bfloat16)
    table_one = radial_one[:, None, :] * embedding.astype(jnp.float32)[None, :, :]
    stencils = jnp.arange(27, dtype=jnp.int32)

    def frame_of(stencil):
        return pair_frame(stencil, positions, shifted(positions, stencil), counts, shifted(counts, stencil), pair_list, shifted(pair_list, stencil))

    def layer_one(running, stencil):
        separation, scaled, weight = frame_of(stencil)
        radial_basis = radial_terms(scaled, weight, orders).astype(jnp.bfloat16)
        return (running + product('xyzkij,xyzjs->xyzkis', radial_basis, shifted(own_kinds, stencil)), None)
    tally_init = jnp.zeros(species.shape[:3] + (orders, slot_total, species_total), jnp.float32)
    tally, _ = lax.scan(layer_one, tally_init, stencils)
    first_message = product('xyzkis,ksc->xyzic', tally, table_one)
    first_gate = product('xyzic,cd->xyzid', first_message.astype(jnp.bfloat16), mix_one)
    hidden = (base_features.astype(jnp.float32) + jax.nn.silu(first_gate)).astype(jnp.bfloat16)

    def layer_sum(field):

        def accumulate(running, stencil):
            separation, scaled, weight = frame_of(stencil)
            radial_basis = radial_terms(scaled, weight, orders).astype(jnp.bfloat16)
            gathered = product('xyzkij,xyzjc->xyzkic', radial_basis, shifted(field, stencil))
            return (running + lax.optimization_barrier(jnp.sum(gathered * radial_two.astype(jnp.float32)[:, None, :], axis=-3)), None)
        summed, _ = lax.scan(accumulate, jnp.zeros(field.shape, jnp.float32), stencils)
        return summed
    second_message = layer_sum(hidden)
    second_gate = product('xyzic,cd->xyzid', second_message.astype(jnp.bfloat16), mix_two)
    upstream = own_live[..., None] * readout
    second_grad = (upstream * silu_slope(second_gate)).astype(jnp.bfloat16)
    message_grad = product('xyzid,cd->xyzic', second_grad, mix_two).astype(jnp.bfloat16)
    hidden_grad = upstream + layer_sum(message_grad)
    first_grad = (hidden_grad * silu_slope(first_gate)).astype(jnp.bfloat16)
    first_message_grad = product('xyzid,cd->xyzic', first_grad, mix_one)
    projected = product('xyzic,ksc->xyzksi', first_message_grad, table_one).astype(jnp.bfloat16)
    radial_wide = radial_two.astype(jnp.float32)[:, None, :]
    weighted_grad = (radial_wide * message_grad.astype(jnp.float32)[..., None, :, :]).astype(jnp.bfloat16)
    weighted_hidden = (radial_wide * hidden.astype(jnp.float32)[..., None, :, :]).astype(jnp.bfloat16)

    def gradient_pass(running, stencil):
        separation, scaled, weight = frame_of(stencil)
        pair_grad = product('xyzkic,xyzjc->xyzkij', weighted_grad, shifted(hidden, stencil))
        pair_grad = pair_grad + product('xyzkic,xyzjc->xyzkij', weighted_hidden, shifted(message_grad, stencil))
        pair_grad = pair_grad + product('xyzksi,xyzjs->xyzkij', projected, shifted(own_kinds, stencil))
        pair_grad = pair_grad + product('xyzksj,xyzis->xyzkij', shifted(projected, stencil), own_kinds)
        strength = lax.optimization_barrier(jnp.sum(pair_grad * radial_slope(scaled, weight, orders), axis=-3))
        return (running + product('xyzij,xyzdij->xyzdi', strength, separation), None)
    summed, _ = lax.scan(gradient_pass, jnp.zeros(positions.shape, jnp.float32), stencils)
    return 2.0 / (REACH * REACH) * summed

def reference(positions, velocities, forces, noise, species, counts, pair_list, masses, embedding, radial_one, mix_one, radial_two, mix_two, readout):
    species_total = masses.shape[0]
    kinds_float = (species[..., None] == jnp.arange(species_total, dtype=jnp.int32)).astype(jnp.float32)
    atom_mass = product('xyzas,s->xyza', kinds_float, masses)[..., None, :]
    half_velocity = velocities + HALF_STEP * forces / atom_mass
    half_position = positions + HALF_STEP * half_velocity
    mixed_velocity = DECAY * half_velocity + jnp.sqrt((1.0 - DECAY * DECAY) / atom_mass) * noise
    new_positions = half_position + HALF_STEP * mixed_velocity
    new_forces = force_field(new_positions, species, counts, pair_list, embedding, radial_one, mix_one, radial_two, mix_two, readout)
    new_velocities = mixed_velocity + HALF_STEP * new_forces / atom_mass
    return (new_positions, new_velocities, new_forces)
```

```python
import functools
import math

import jax
import jax.numpy as jnp
from jax import lax
from jax.experimental import pallas as pl
from jax.experimental.pallas import tpu as pltpu
from jax.sharding import PartitionSpec as P

SIDE = 10.0
REACH = 5.0
HALF_STEP = 0.25
DECAY = math.exp(-0.5)
FAR = 1.0e4

ORDERS = 8
KINDS = 8
SLOTS = 128
COLUMN = 3
ATOMS = COLUMN * SLOTS
CHANNELS = 128
PARTS = 7
CHUNK = 32

F32 = jnp.float32
BF16 = jnp.bfloat16
HIGHEST = lax.Precision.HIGHEST
ODD = (3.14159265160, -5.16771249, 2.55012026, -0.59890223, 0.07772681)
EVEN = (1.0, -4.93480219, 4.05869615, -1.33500654, 0.23347127, -0.02380946)


def fit_terms():
    import numpy as np

    nodes = 0.5 * np.cos(np.pi * (np.arange(400) + 0.5) / 800)
    odd = np.polynomial.polynomial.polyfit(nodes * nodes, np.sin(np.pi * nodes) / nodes, 4)
    even = np.polynomial.polynomial.polyfit(nodes * nodes, np.cos(np.pi * nodes), 4)
    return tuple(float(value) for value in odd), tuple(float(value) for value in even)


ODD, EVEN = fit_terms()


def horner(terms, square):
    total = terms[-1]
    for term in terms[-2::-1]:
        total = total * square + term
    return total


def turned(row):
    return jnp.broadcast_to(row, (SLOTS, SLOTS)).T


def dot(left, right, contract=((1,), (0,)), precision=None):
    return lax.dot_general(
        left, right, (contract, ((), ())), precision=precision, preferred_element_type=F32
    )


def spread_own(own_ref, own_cols):
    for block in range(COLUMN):
        for axis in range(3):
            own_cols[axis, pl.ds(block * SLOTS, SLOTS), :] = turned(
                own_ref[0, block, axis : axis + 1, :] * (1.0 / REACH)
            )


def mark_diagonal(column, diagonal):
    rows = lax.broadcasted_iota(jnp.int32, (SLOTS, SLOTS), 0)
    lanes = lax.broadcasted_iota(jnp.int32, (SLOTS, SLOTS), 1)
    hit = jnp.logical_and(rows == lanes, column == 4)
    diagonal[...] = jnp.where(hit, FAR * FAR, 0.0)


def offset_z(block, near):
    return (near - block + 1) % 3 - 1


def near_rows(lists_ref, near_ref, column, block, near):
    step_x = column // 3 - 1
    step_y = column % 3 - 1
    step_z = offset_z(block, near)
    stencil = column * 3 + step_z + 1
    ahead = lists_ref[4, block, jnp.clip(stencil - 14, 0, 12)]
    behind = lists_ref[column, near, jnp.clip(12 - stencil, 0, 12)]
    listed = jnp.where(stencil == 13, 1.0, jnp.where(stencil > 13, ahead, behind))
    slots = lax.broadcasted_iota(jnp.int32, (1, SLOTS), 1).astype(F32)
    live = slots < near_ref[0, near, 4:5, :]
    x = (near_ref[0, near, 0:1, :] + SIDE * step_x.astype(F32)) * (1.0 / REACH)
    y = (near_ref[0, near, 1:2, :] + SIDE * step_y.astype(F32)) * (1.0 / REACH)
    z = (near_ref[0, near, 2:3, :] + SIDE * step_z) * (1.0 / REACH)
    x = jnp.where(jnp.logical_and(live, listed > 0.5), x, FAR)
    return x, y, z


def left_over(rows, own_cols, diagonal, block, near, start):
    span = pl.ds(block * SLOTS + start, CHUNK)
    dx = rows[0] - own_cols[0, span, :]
    dy = rows[1] - own_cols[1, span, :]
    dz = rows[2] - own_cols[2, span, :]
    square = dx * dx + dy * dy + dz * dz
    if near == block:
        square = square + diagonal[pl.ds(start, CHUNK), :]
    return jnp.maximum(1.0 - square, 0.0), (dx, dy, dz)


def species_features(near_ref, embedding, near):
    kinds = turned(near_ref[0, near, 3:4, :])
    lanes = lax.broadcasted_iota(jnp.int32, (SLOTS, SLOTS), 1).astype(F32)
    one_hot = jnp.where(kinds == lanes, 1.0, 0.0).astype(BF16)
    return dot(one_hot, embedding).astype(BF16)


def basis_kernel(
    lists_ref, own_ref, near_ref, embedding_ref, radial_ref, mix_ref,
    basis_ref, hidden_ref, gate_ref,
    own_cols, diagonal, message, base, features,
):
    column = pl.program_id(0)

    @pl.when(column == 0)
    def _():
        spread_own(own_ref, own_cols)
        message[...] = jnp.zeros_like(message)
        for block in range(COLUMN):
            base[pl.ds(block * SLOTS, SLOTS), :] = species_features(
                own_ref, embedding_ref[...], block
            )

    mark_diagonal(column, diagonal)
    for block in range(COLUMN):
        for near in range(COLUMN):
            rows = near_rows(lists_ref, near_ref, column, block, near)
            for start in range(0, SLOTS, CHUNK):
                left, _ = left_over(rows, own_cols, diagonal, block, near, start)
                middle = left - 0.5
                cosine = middle * horner(ODD, middle * middle)
                twice = cosine + cosine
                last = left * left
                now = last * cosine
                span = (pl.ds(block * SLOTS + start, CHUNK), pl.ds(near * SLOTS, SLOTS))
                basis_ref[0, 0, span[0], span[1]] = last.astype(BF16)
                basis_ref[0, 1, span[0], span[1]] = now.astype(BF16)
                for order in range(2, ORDERS):
                    last, now = now, twice * now - last
                    basis_ref[0, order, span[0], span[1]] = now.astype(BF16)
    for near in range(COLUMN):
        features[pl.ds(near * SLOTS, SLOTS), :] = species_features(
            near_ref, embedding_ref[...], near
        )
    total = message[...]
    for order in range(ORDERS):
        total = total + radial_ref[order : order + 1, :] * dot(basis_ref[0, order], features[...])
    message[...] = total

    @pl.when(column == 8)
    def _():
        gate = dot(message[...].astype(BF16), mix_ref[...])
        gate_ref[...] = gate
        hidden_ref[...] = (base[...].astype(F32) + gate * jax.nn.sigmoid(gate)).astype(BF16)


def silu_slope(values):
    sigmoid = jax.nn.sigmoid(values)
    return sigmoid * (1.0 + values * (1.0 - sigmoid))


def upstream_of(counts_ref, readout_ref):
    slots = lax.broadcasted_iota(jnp.int32, (SLOTS, CHANNELS), 0)
    readout = jnp.broadcast_to(readout_ref[...], (SLOTS, CHANNELS))
    return jnp.concatenate(
        [jnp.where(slots < counts_ref[block], readout, 0.0) for block in range(COLUMN)], axis=0
    )


def gather_message(basis_ref, field_ref, radial_ref, message):
    @pl.when(pl.program_id(0) == 0)
    def _():
        message[...] = jnp.zeros_like(message)

    total = message[...]
    for order in range(ORDERS):
        total = total + radial_ref[order : order + 1, :] * dot(basis_ref[0, order], field_ref[0])
    message[...] = total


def second_kernel(
    counts_ref, basis_ref, hidden_ref, radial_ref, mix_ref, readout_ref, grad_ref, message
):
    gather_message(basis_ref, hidden_ref, radial_ref, message)

    @pl.when(pl.program_id(0) == 8)
    def _():
        gate = dot(message[...].astype(BF16), mix_ref[...])
        second = (upstream_of(counts_ref, readout_ref) * silu_slope(gate)).astype(BF16)
        grad_ref[...] = dot(second, mix_ref[...], ((1,), (1,))).astype(BF16)


def first_kernel(
    counts_ref, basis_ref, grad_ref, radial_ref, mix_ref, readout_ref, gate_ref, table_ref,
    projected_ref, message,
):
    gather_message(basis_ref, grad_ref, radial_ref, message)

    @pl.when(pl.program_id(0) == 8)
    def _():
        hidden_grad = upstream_of(counts_ref, readout_ref) + message[...]
        first = (hidden_grad * silu_slope(gate_ref[...])).astype(BF16)
        message_grad = dot(first, mix_ref[...], ((1,), (1,)))
        projected_ref[...] = dot(
            table_ref[...], message_grad, ((1,), (1,)), HIGHEST
        ).astype(BF16)


def split(values):
    high = values.astype(BF16)
    return high, (values - high.astype(F32)).astype(BF16)


def slope_kernel(
    lists_ref, own_ref, near_ref, slope_ref, kind_ref, own_cols, diagonal, table
):
    column = pl.program_id(0)

    @pl.when(column == 0)
    def _():
        spread_own(own_ref, own_cols)
        kind_ref[...] = jnp.zeros_like(kind_ref)

    mark_diagonal(column, diagonal)
    for block in range(COLUMN):
        for near in range(COLUMN):
            rows = near_rows(lists_ref, near_ref, column, block, near)
            for start in range(0, SLOTS, CHUNK):
                left, _ = left_over(rows, own_cols, diagonal, block, near, start)
                middle = left - 0.5
                square = middle * middle
                cosine = middle * horner(ODD, square)
                sine = horner(EVEN, square)
                twice = cosine + cosine
                last_a = -2.0 * left
                now_a = last_a * cosine
                now_b = (left * left) * (sine * -math.pi)
                last_b = None
                span = (pl.ds(block * SLOTS + start, CHUNK), pl.ds(near * SLOTS, SLOTS))
                slope_ref[0, 0, span[0], span[1]] = last_a.astype(BF16)
                slope_ref[0, 1, span[0], span[1]] = (now_a + now_b).astype(BF16)
                for order in range(2, ORDERS):
                    last_a, now_a = now_a, twice * now_a - last_a
                    if last_b is None:
                        last_b, now_b = now_b, twice * now_b
                    else:
                        last_b, now_b = now_b, twice * now_b - last_b
                    slope_ref[0, order, span[0], span[1]] = (
                        now_a + float(order) * now_b
                    ).astype(BF16)
    for block in range(COLUMN):
        for near in range(COLUMN):
            coordinates = true_rows(near_ref, column, block, near)
            one_hot = kind_rows(near_ref, near)
            fill_table(table, one_hot, coordinates, near)
        for order in range(ORDERS):
            kind_ref[order, pl.ds(block * SLOTS, SLOTS), :] += dot(
                slope_ref[0, order, pl.ds(block * SLOTS, SLOTS), :], table[...], ((1,), (1,))
            )


def true_rows(near_ref, column, block, near):
    steps = (
        (column // 3 - 1).astype(F32),
        (column % 3 - 1).astype(F32),
        float(offset_z(block, near)),
    )
    return [
        (near_ref[0, near, axis : axis + 1, :] + SIDE * steps[axis]) * (1.0 / REACH)
        for axis in range(3)
    ]


def kind_rows(near_ref, near):
    kinds = lax.broadcasted_iota(jnp.int32, (KINDS, SLOTS), 0).astype(F32)
    return jnp.where(near_ref[0, near, 3:4, :] == kinds, 1.0, 0.0)


def fill_table(table, values, coordinates, near):
    pieces = [values.astype(BF16)]
    for axis in range(3):
        pieces.extend(split(values * coordinates[axis]))
    pieces.append(jnp.zeros((SLOTS - KINDS * PARTS, SLOTS), BF16))
    pieces = [piece.astype(F32) for piece in pieces]
    table[:, pl.ds(near * SLOTS, SLOTS)] = jnp.concatenate(pieces, axis=0).astype(BF16)


def pair_kernel(
    lists_ref, own_ref, near_ref, slope_ref, near_hidden_ref, near_grad_ref, hidden_ref, grad_ref,
    radial_ref, force_ref, own_cols, left_side, right_side,
):
    column = pl.program_id(0)

    @pl.when(column == 0)
    def _():
        spread_own(own_ref, own_cols)
        force_ref[...] = jnp.zeros_like(force_ref)
        for order in range(ORDERS):
            radial = radial_ref[order : order + 1, :]
            left_side[order, :, 0:CHANNELS] = (radial * grad_ref[0].astype(F32)).astype(BF16)
            left_side[order, :, CHANNELS : 2 * CHANNELS] = (
                radial * hidden_ref[0].astype(F32)
            ).astype(BF16)

    right_side[:, 0:CHANNELS] = near_hidden_ref[0]
    right_side[:, CHANNELS : 2 * CHANNELS] = near_grad_ref[0]
    for block in range(COLUMN):
        span = pl.ds(block * SLOTS, SLOTS)
        strength = jnp.zeros((SLOTS, ATOMS), F32)
        for order in range(ORDERS):
            pair = dot(left_side[order, span, :], right_side[...], ((1,), (1,)))
            strength = strength + pair * slope_ref[0, order, span, :].astype(F32)
        for near in range(COLUMN):
            rows = true_rows(near_ref, column, block, near)
            part = strength[:, near * SLOTS : (near + 1) * SLOTS]
            for axis in range(3):
                force_ref[axis, span, :] += part * (rows[axis] - own_cols[axis, span, :])


def last_kernel(
    counts_ref, slope_ref, projected_ref, own_projected_ref, own_ref, near_ref, force_ref,
    kind_ref, mixed_ref, mass_ref, new_force_ref, new_velocity_ref, own_cols, table, near_kind,
):
    column = pl.program_id(0)

    @pl.when(column == 0)
    def _():
        spread_own(own_ref, own_cols)
        near_kind[...] = jnp.zeros_like(near_kind)

    for block in range(COLUMN):
        span = pl.ds(block * SLOTS, SLOTS)
        total = near_kind[span, :]
        for order in range(ORDERS):
            for near in range(COLUMN):
                values = projected_ref[
                    0, order * KINDS : (order + 1) * KINDS, near * SLOTS : (near + 1) * SLOTS
                ].astype(F32)
                fill_table(table, values, true_rows(near_ref, column, block, near), near)
            total = total + dot(slope_ref[0, order, span, :], table[...], ((1,), (1,)))
        near_kind[span, :] = total

    @pl.when(column == 8)
    def _():
        lanes = lax.broadcasted_iota(jnp.int32, (SLOTS, SLOTS), 1)
        lane_kind = (lanes % KINDS).astype(F32)
        part = lanes // KINDS
        inner = lax.broadcasted_iota(jnp.int32, (ORDERS * KINDS, SLOTS), 0)
        outer = lax.broadcasted_iota(jnp.int32, (ORDERS * KINDS, SLOTS), 1) % KINDS
        slots = lax.broadcasted_iota(jnp.int32, (1, SLOTS), 1)
        for block in range(COLUMN):
            span = pl.ds(block * SLOTS, SLOTS)
            kinds = turned(own_ref[0, block, 3:4, :])
            total = jnp.where(kinds == lane_kind, near_kind[span, :], 0.0)
            own = own_projected_ref[0, :, span]
            for order in range(ORDERS):
                pick = jnp.where(inner == outer + order * KINDS, 1.0, 0.0).astype(BF16)
                spread = dot(own, pick, ((0,), (0,)))
                total = total + spread * kind_ref[order, span, :]
            for axis in range(3):
                here = jnp.logical_or(part == 1 + 2 * axis, part == 2 + 2 * axis)
                factor = jnp.where(here, 1.0, jnp.where(part == 0, -own_cols[axis, span, :], 0.0))
                lanes_force = force_ref[axis, span, :] + total * factor
                summed = jnp.sum(lanes_force.T, axis=0, keepdims=True)
                live = slots < counts_ref[block]
                force = jnp.where(live, summed * (2.0 / REACH), 0.0)
                new_force_ref[block, axis : axis + 1, :] = force
                new_velocity_ref[block, axis : axis + 1, :] = (
                    mixed_ref[block, axis : axis + 1, :]
                    + HALF_STEP * force / mass_ref[block : block + 1, :]
                )


def neighbours(cell):
    count_x, count_y = lax.axis_size("gx"), lax.axis_size("gy")
    row = jnp.stack(
        [
            lax.ppermute(cell, "gy", [(i, (i + 1) % count_y) for i in range(count_y)]),
            cell,
            lax.ppermute(cell, "gy", [((i + 1) % count_y, i) for i in range(count_y)]),
        ]
    )
    return jnp.concatenate(
        [
            lax.ppermute(row, "gx", [(i, (i + 1) % count_x) for i in range(count_x)]),
            row,
            lax.ppermute(row, "gx", [((i + 1) % count_x, i) for i in range(count_x)]),
        ]
    )


SMEM = pl.BlockSpec(memory_space=pltpu.SMEM)


def whole(*shape):
    return pl.BlockSpec(shape, lambda column: (0,) * len(shape))


def at_column(*shape):
    return pl.BlockSpec((1,) + shape, lambda column: (column,) + (0,) * len(shape))


def at_centre(*shape):
    return pl.BlockSpec((1,) + shape, lambda column: (4,) + (0,) * len(shape))


def call(kernel, name, out_shape, in_specs, out_specs, scratch, flops, bytes_accessed):
    return pl.pallas_call(
        kernel,
        name=name,
        out_shape=out_shape,
        grid=(9,),
        in_specs=in_specs,
        out_specs=out_specs,
        scratch_shapes=scratch,
        cost_estimate=pl.CostEstimate(
            flops=flops, bytes_accessed=bytes_accessed, transcendentals=0
        ),
        compiler_params=pltpu.CompilerParams(dimension_semantics=("arbitrary",)),
    )


def shape_of(*shape, kind=F32):
    return jax.ShapeDtypeStruct(shape, kind)


PAIR_BYTES = 9 * ORDERS * ATOMS * ATOMS * 2
PAIR_FLOPS = 9 * ORDERS * ATOMS * ATOMS * CHANNELS * 2


def force_field(
    positions, species, counts, pair_list, embedding, radial_one, mix_one, radial_two, mix_two,
    readout, mixed_velocity, atom_mass,
):
    geometry = jnp.concatenate(
        [
            positions,
            species.astype(F32)[:, None, :],
            jnp.broadcast_to(counts.astype(F32)[:, None, None], (COLUMN, 1, SLOTS)),
            jnp.pad(pair_list.astype(F32)[:, None, :], ((0, 0), (0, 0), (0, SLOTS - 13))),
            jnp.zeros((COLUMN, 2, SLOTS), F32),
        ],
        axis=1,
    )
    near_geometry = neighbours(geometry)
    lists = near_geometry[:, :, 5, :13]
    kinds = embedding.shape[0]
    wide_embedding = jnp.pad(embedding, ((0, SLOTS - kinds), (0, 0)))
    table = (
        radial_one[:, None, :]
        * jnp.pad(embedding.astype(F32), ((0, KINDS - kinds), (0, 0)))[None, :, :]
    ).reshape(ORDERS * KINDS, CHANNELS)
    radial_wide = radial_two.astype(F32)
    readout_row = readout[None, :]

    cols = pltpu.VMEM((3, ATOMS, SLOTS), F32)
    message = pltpu.VMEM((ATOMS, CHANNELS), F32)
    square = pltpu.VMEM((SLOTS, SLOTS), F32)
    pairs = (ORDERS, ATOMS, ATOMS)
    geometry_specs = [SMEM, at_centre(COLUMN, 8, SLOTS), at_column(COLUMN, 8, SLOTS)]

    basis, hidden, first_gate = call(
        basis_kernel,
        "basis",
        (
            shape_of(9, *pairs, kind=BF16),
            shape_of(ATOMS, CHANNELS, kind=BF16),
            shape_of(ATOMS, CHANNELS),
        ),
        geometry_specs + [whole(SLOTS, CHANNELS), whole(ORDERS, CHANNELS), whole(CHANNELS, CHANNELS)],
        (at_column(*pairs), whole(ATOMS, CHANNELS), whole(ATOMS, CHANNELS)),
        [
            cols, square, message, pltpu.VMEM((ATOMS, CHANNELS), BF16),
            pltpu.VMEM((ATOMS, CHANNELS), BF16),
        ],
        PAIR_FLOPS,
        PAIR_BYTES,
    )(lists, near_geometry, near_geometry, wide_embedding, radial_one, mix_one)
    near_hidden = neighbours(hidden)

    slope, kind_sums = call(
        slope_kernel,
        "slope",
        (shape_of(9, *pairs, kind=BF16), shape_of(ORDERS, ATOMS, SLOTS)),
        geometry_specs,
        (at_column(*pairs), whole(ORDERS, ATOMS, SLOTS)),
        [cols, square, pltpu.VMEM((SLOTS, ATOMS), BF16)],
        PAIR_FLOPS,
        PAIR_BYTES,
    )(lists, near_geometry, near_geometry)

    message_grad = call(
        second_kernel,
        "second",
        shape_of(ATOMS, CHANNELS, kind=BF16),
        [
            SMEM, at_column(*pairs), at_column(ATOMS, CHANNELS), whole(ORDERS, CHANNELS),
            whole(CHANNELS, CHANNELS), whole(1, CHANNELS),
        ],
        whole(ATOMS, CHANNELS),
        [message],
        PAIR_FLOPS,
        PAIR_BYTES,
    )(counts, basis, near_hidden, radial_wide, mix_two, readout_row)
    near_grad = neighbours(message_grad)

    projected = call(
        first_kernel,
        "first",
        shape_of(ORDERS * KINDS, ATOMS, kind=BF16),
        [
            SMEM, at_column(*pairs), at_column(ATOMS, CHANNELS), whole(ORDERS, CHANNELS),
            whole(CHANNELS, CHANNELS), whole(1, CHANNELS), whole(ATOMS, CHANNELS),
            whole(ORDERS * KINDS, CHANNELS),
        ],
        whole(ORDERS * KINDS, ATOMS),
        [message],
        PAIR_FLOPS,
        PAIR_BYTES,
    )(counts, basis, near_grad, radial_wide, mix_one, readout_row, first_gate, table)
    near_projected = neighbours(projected)

    partial_force = call(
        pair_kernel,
        "pair",
        shape_of(3, ATOMS, SLOTS),
        geometry_specs
        + [
            at_column(*pairs), at_column(ATOMS, CHANNELS), at_column(ATOMS, CHANNELS),
            at_centre(ATOMS, CHANNELS), at_centre(ATOMS, CHANNELS), whole(ORDERS, CHANNELS),
        ],
        whole(3, ATOMS, SLOTS),
        [
            cols, pltpu.VMEM((ORDERS, ATOMS, 2 * CHANNELS), BF16),
            pltpu.VMEM((ATOMS, 2 * CHANNELS), BF16),
        ],
        2 * PAIR_FLOPS,
        PAIR_BYTES,
    )(
        lists, near_geometry, near_geometry, slope, near_hidden, near_grad, near_hidden, near_grad,
        radial_wide,
    )

    return call(
        last_kernel,
        "last",
        (shape_of(COLUMN, 3, SLOTS), shape_of(COLUMN, 3, SLOTS)),
        [
            SMEM, at_column(*pairs), at_column(ORDERS * KINDS, ATOMS),
            at_centre(ORDERS * KINDS, ATOMS), at_centre(COLUMN, 8, SLOTS),
            at_column(COLUMN, 8, SLOTS), whole(3, ATOMS, SLOTS), whole(ORDERS, ATOMS, SLOTS),
            whole(COLUMN, 3, SLOTS), whole(COLUMN, SLOTS),
        ],
        (whole(COLUMN, 3, SLOTS), whole(COLUMN, 3, SLOTS)),
        [cols, pltpu.VMEM((SLOTS, ATOMS), BF16), pltpu.VMEM((ATOMS, SLOTS), F32)],
        PAIR_FLOPS,
        PAIR_BYTES,
    )(
        counts, slope, near_projected, near_projected, near_geometry, near_geometry, partial_force,
        kind_sums, mixed_velocity, atom_mass,
    )


def on_device(
    positions, velocities, forces, noise, species, counts, pair_list, masses, embedding,
    radial_one, mix_one, radial_two, mix_two, readout,
):
    positions, velocities, forces, noise, species, counts, pair_list = (
        value[0, 0]
        for value in (positions, velocities, forces, noise, species, counts, pair_list)
    )
    atom_mass = jnp.zeros(species.shape, F32)
    for kind in range(masses.shape[0]):
        atom_mass = jnp.where(species == kind, masses[kind], atom_mass)
    wide_mass = atom_mass[:, None, :]
    half_velocity = velocities + HALF_STEP * forces / wide_mass
    half_position = positions + HALF_STEP * half_velocity
    mixed_velocity = DECAY * half_velocity + jnp.sqrt((1.0 - DECAY * DECAY) / wide_mass) * noise
    new_positions = half_position + HALF_STEP * mixed_velocity
    new_forces, new_velocities = force_field(
        new_positions, species, counts, pair_list, embedding, radial_one, mix_one, radial_two,
        mix_two, readout, mixed_velocity, atom_mass,
    )
    return tuple(value[None, None] for value in (new_positions, new_velocities, new_forces))


def solution(mesh):
    split_spec = P("gx", "gy")
    return jax.shard_map(
        on_device,
        mesh=mesh,
        in_specs=(split_spec,) * 7 + (P(),) * 7,
        out_specs=(split_spec,) * 3,
        check_vma=False,
    )
```

```python
import functools
import math

import jax
import jax.numpy as jnp
from jax import lax
from jax.experimental import pallas as pl
from jax.experimental.pallas import tpu as pltpu
from jax.sharding import PartitionSpec as P

SIDE = 10.0
REACH = 5.0
HALF_STEP = 0.25
DECAY = math.exp(-0.5)
FAR = 1.0e4

ORDERS = 8
KINDS = 8
SLOTS = 128
COLUMN = 3
ATOMS = COLUMN * SLOTS
CHANNELS = 128
PARTS = 9
CHUNK = 32
OUTER = -1
LIMIT = 12 * 2**20

F32 = jnp.float32
BF16 = jnp.bfloat16
HIGHEST = lax.Precision.HIGHEST
ODD = (3.14159265160, -5.16771249, 2.55012026, -0.59890223, 0.07772681)
EVEN = (1.0, -4.93480219, 4.05869615, -1.33500654, 0.23347127, -0.02380946)


def fit_terms():
    import numpy as np

    nodes = 0.5 * np.cos(np.pi * (np.arange(400) + 0.5) / 800)
    odd = np.polynomial.polynomial.polyfit(nodes * nodes, np.sin(np.pi * nodes) / nodes, 4)
    even = np.polynomial.polynomial.polyfit(nodes * nodes, np.cos(np.pi * nodes), 4)
    return tuple(float(value) for value in odd), tuple(float(value) for value in even)


ODD, EVEN = fit_terms()


def horner(terms, square):
    total = terms[-1]
    for term in terms[-2::-1]:
        total = total * square + term
    return total


def turned(row):
    return jnp.broadcast_to(row, (SLOTS, SLOTS)).T


def dot(left, right, contract=((1,), (0,)), precision=None):
    return lax.dot_general(
        left, right, (contract, ((), ())), precision=precision, preferred_element_type=F32
    )


def spread_own(own_ref, own_cols):
    for block in range(COLUMN):
        for axis in range(3):
            own_cols[axis, pl.ds(block * SLOTS, SLOTS), :] = turned(
                own_ref[0, block, axis : axis + 1, :] * (1.0 / REACH)
            )


def mark_diagonal(column, diagonal):
    rows = lax.broadcasted_iota(jnp.int32, (SLOTS, SLOTS), 0)
    lanes = lax.broadcasted_iota(jnp.int32, (SLOTS, SLOTS), 1)
    hit = jnp.logical_and(rows == lanes, column == 4)
    diagonal[...] = jnp.where(hit, FAR * FAR, 0.0)


def offset_z(block, near):
    return (near - block + 1) % 3 - 1


def place_of(part):
    step = pl.program_id(0)
    if part == OUTER:
        return step + 3 * (step // 3)
    return step + 3 * part


def mark_listed(own_ref, near_ref, column, picked, listed):
    lanes = lax.broadcasted_iota(jnp.int32, (1, SLOTS), 1)
    for block in range(COLUMN):
        for near in range(COLUMN):
            stencil = column * 3 + offset_z(block, near) + 1
            ahead = jnp.where(lanes == stencil - 14, own_ref[0, block, 5:6, :], 0.0)
            behind = jnp.where(lanes == 12 - stencil, near_ref[0, near, 5:6, :], 0.0)
            own = jnp.where(lanes == jnp.where(stencil == 13, 0, -1), 1.0, 0.0)
            row = block * COLUMN + near
            picked[row : row + 1, :] = own + ahead + behind
    sums = jnp.sum(picked[...], axis=1, keepdims=True)
    listed[...] = jnp.broadcast_to(sums, listed.shape)


def near_rows(listed, near_ref, column, block, near):
    x, y, z = true_rows(near_ref, column, near)
    z = z + (SIDE / REACH) * offset_z(block, near)
    slots = lax.broadcasted_iota(jnp.int32, (1, SLOTS), 1).astype(F32)
    row = block * COLUMN + near
    counts = jnp.logical_and(
        slots < near_ref[0, near, 4:5, :], listed[row : row + 1, :] > 0.5
    )
    return jnp.where(counts, x, FAR), y, z


def left_over(rows, own_cols, diagonal, block, near, start):
    span = pl.ds(block * SLOTS + start, CHUNK)
    dx = rows[0] - own_cols[0, span, :]
    dy = rows[1] - own_cols[1, span, :]
    dz = rows[2] - own_cols[2, span, :]
    square = dx * dx + dy * dy + dz * dz
    if near == block:
        square = square + diagonal[pl.ds(start, CHUNK), :]
    return jnp.maximum(1.0 - square, 0.0)


def species_features(near_ref, embedding, near):
    kinds = turned(near_ref[0, near, 3:4, :])
    lanes = lax.broadcasted_iota(jnp.int32, (SLOTS, SLOTS), 1).astype(F32)
    one_hot = jnp.where(kinds == lanes, 1.0, 0.0).astype(BF16)
    return dot(one_hot, embedding).astype(BF16)


def basis_kernel(part, own_ref, *refs):
    if part == OUTER:
        near_0, near_2, embedding_ref, radial_ref, mix_ref, before_ref = refs[:6]
        basis_ref, hidden_ref, gate_ref = refs[6:9]
        fields = (near_0, near_2)
    else:
        near_1, embedding_ref, radial_ref, basis_ref, after_ref = refs[:5]
        fields = (near_1,)
    own_cols, near_ref, diagonal, picked, listed, message, features = refs[-7:]
    column = place_of(part)
    near_ref[0] = pick(fields)

    @pl.when(pl.program_id(0) == 0)
    def _():
        spread_own(own_ref, own_cols)
        picked[...] = jnp.zeros_like(picked)
        if part == OUTER:
            message[...] = before_ref[...]
        else:
            message[...] = jnp.zeros_like(message)

    mark_diagonal(column, diagonal)
    mark_listed(own_ref, near_ref, column, picked, listed)
    for near in range(COLUMN):
        features[pl.ds(near * SLOTS, SLOTS), :] = species_features(
            near_ref, embedding_ref[...].astype(BF16), near
        )
    for block in range(COLUMN):
        for near in range(COLUMN):
            rows = near_rows(listed, near_ref, column, block, near)
            for start in range(0, SLOTS, CHUNK):
                left = left_over(rows, own_cols, diagonal, block, near, start)
                middle = left - 0.5
                cosine = middle * horner(ODD, middle * middle)
                twice = cosine + cosine
                last = left * left
                now = last * cosine
                span = (
                    pl.ds(block * SLOTS + start, CHUNK),
                    pl.ds(near * SLOTS, SLOTS),
                )
                basis_ref[0, 0, span[0], span[1]] = last.astype(BF16)
                basis_ref[0, 1, span[0], span[1]] = now.astype(BF16)
                for order in range(2, ORDERS):
                    last, now = now, twice * now - last
                    basis_ref[0, order, span[0], span[1]] = now.astype(BF16)
    gathered = dot(basis_ref[0].reshape(ORDERS * ATOMS, ATOMS), features[...])
    add_orders(gathered, radial_ref, message)

    @pl.when(pl.program_id(0) == pl.num_programs(0) - 1)
    def _():
        if part == OUTER:
            gate = dot(message[...].astype(BF16), mix_ref[...].astype(BF16))
            gate_ref[...] = gate
            base = jnp.concatenate(
                [species_features(own_ref, embedding_ref[...].astype(BF16), block) for block in range(COLUMN)]
            )
            hidden_ref[...] = (base.astype(F32) + gate * jax.nn.sigmoid(gate)).astype(BF16)
        else:
            after_ref[...] = message[...]


def silu_slope(values):
    sigmoid = jax.nn.sigmoid(values)
    return sigmoid * (1.0 + values * (1.0 - sigmoid))


def pick(refs):
    if len(refs) == 1:
        return refs[0][0]
    return jnp.where(pl.program_id(0) < 3, refs[0][0], refs[1][0])


def add_orders(gathered, radial_ref, message):
    total = message[...]
    for order in range(ORDERS):
        rows = gathered[order * ATOMS : (order + 1) * ATOMS, :]
        total = total + radial_ref[order : order + 1, :] * rows
    message[...] = total


def gather_kernel(basis_ref, field_ref, radial_ref, after_ref, message):
    @pl.when(pl.program_id(0) == 0)
    def _():
        message[...] = jnp.zeros_like(message)

    gathered = dot(basis_ref[0].reshape(ORDERS * ATOMS, ATOMS), field_ref[0])
    add_orders(gathered, radial_ref, message)

    @pl.when(pl.program_id(0) == 2)
    def _():
        after_ref[...] = message[...]


def gather_outer(basis_ref, fields, radial_ref, before_ref, message):
    @pl.when(pl.program_id(0) == 0)
    def _():
        message[...] = before_ref[...]

    gathered = dot(basis_ref[0].reshape(ORDERS * ATOMS, ATOMS), pick(fields))
    add_orders(gathered, radial_ref, message)


def second_kernel(
    basis_ref, hidden_0, hidden_2, radial_ref, mix_ref, upstream_ref, before_ref, grad_ref, message
):
    gather_outer(basis_ref, (hidden_0, hidden_2), radial_ref, before_ref, message)

    @pl.when(pl.program_id(0) == 5)
    def _():
        gate = dot(message[...].astype(BF16), mix_ref[...].astype(BF16))
        second = (upstream_ref[...] * silu_slope(gate)).astype(BF16)
        grad_ref[...] = dot(second, mix_ref[...].astype(BF16), ((1,), (1,))).astype(BF16)


def first_kernel(
    basis_ref, grad_0, grad_2, radial_ref, mix_ref, upstream_ref, gate_ref, table_ref, before_ref,
    projected_ref, message,
):
    gather_outer(basis_ref, (grad_0, grad_2), radial_ref, before_ref, message)

    @pl.when(pl.program_id(0) == 5)
    def _():
        hidden_grad = upstream_ref[...] + message[...]
        first = (hidden_grad * silu_slope(gate_ref[...])).astype(BF16)
        message_grad = dot(first, mix_ref[...].astype(BF16), ((1,), (1,)))
        projected_ref[...] = dot(
            table_ref[...], message_grad, ((1,), (1,)), HIGHEST
        ).astype(BF16)


def start_from(before_ref, total_ref):
    if before_ref is None:
        total_ref[...] = jnp.zeros_like(total_ref)
    else:
        total_ref[...] = before_ref[...]


def slope_kernel(
    group, own_ref, near_ref, *refs
):
    before_ref = None if group == 1 else refs[0]
    slope_ref, kind_ref, own_cols, diagonal, picked, listed, table = refs[-7:]
    column = place_of(group)

    @pl.when(pl.program_id(0) == 0)
    def _():
        spread_own(own_ref, own_cols)
        picked[...] = jnp.zeros_like(picked)
        start_from(before_ref, kind_ref)

    mark_diagonal(column, diagonal)
    mark_listed(own_ref, near_ref, column, picked, listed)
    one_hots = [kind_rows(near_ref, near) for near in range(COLUMN)]
    fill_table(table, one_hots, near_ref, column)
    for block in range(COLUMN):
        for near in range(COLUMN):
            rows = near_rows(listed, near_ref, column, block, near)
            for start in range(0, SLOTS, CHUNK):
                left = left_over(rows, own_cols, diagonal, block, near, start)
                middle = left - 0.5
                square = middle * middle
                cosine = middle * horner(ODD, square)
                sine = horner(EVEN, square)
                twice = cosine + cosine
                last_a = -2.0 * left
                now_a = last_a * cosine
                now_b = (left * left) * (sine * -math.pi)
                last_b = None
                span = (
                    pl.ds(block * SLOTS + start, CHUNK),
                    pl.ds(near * SLOTS, SLOTS),
                )
                slope_ref[0, 0, span[0], span[1]] = last_a.astype(BF16)
                slope_ref[0, 1, span[0], span[1]] = (now_a + now_b).astype(BF16)
                for order in range(2, ORDERS):
                    last_a, now_a = now_a, twice * now_a - last_a
                    if last_b is None:
                        last_b, now_b = now_b, twice * now_b
                    else:
                        last_b, now_b = now_b, twice * now_b - last_b
                    slope_ref[0, order, span[0], span[1]] = (
                        now_a + float(order) * now_b
                    ).astype(BF16)
    sums = dot(slope_ref[0].reshape(ORDERS * ATOMS, ATOMS), table[...], ((1,), (1,)))
    kind_ref[...] += sums.reshape(ORDERS, ATOMS, SLOTS)


def true_rows(near_ref, column, near):
    steps = ((column // 3 - 1).astype(F32), (column % 3 - 1).astype(F32), 0.0)
    return [
        (near_ref[0, near, axis : axis + 1, :] + SIDE * steps[axis]) * (1.0 / REACH)
        for axis in range(3)
    ]


def kind_rows(near_ref, near):
    kinds = lax.broadcasted_iota(jnp.int32, (KINDS, SLOTS), 0).astype(F32)
    return jnp.where(near_ref[0, near, 3:4, :] == kinds, 1.0, 0.0)


def fill_table(table, values, near_ref, column):
    for near in range(COLUMN):
        zero = jnp.zeros((KINDS, SLOTS), F32)
        pieces = [values[near] if part == near else zero for part in range(COLUMN)]
        for row in true_rows(near_ref, column, near):
            product = values[near] * row
            high = product.astype(BF16).astype(F32)
            pieces.extend((high, product - high))
        pieces.extend([zero] * (SLOTS // KINDS - PARTS))
        table[:, pl.ds(near * SLOTS, SLOTS)] = jnp.concatenate(pieces, axis=0).astype(BF16)


def pair_kernel(
    group, own_ref, near_ref, slope_ref, near_hidden_ref, near_grad_ref, hidden_ref, grad_ref,
    radial_ref, *refs,
):
    before_ref = None if group == 1 else refs[0]
    force_ref, own_cols, left_side, right_side = refs[-4:]
    column = place_of(group)

    @pl.when(pl.program_id(0) == 0)
    def _():
        spread_own(own_ref, own_cols)
        start_from(before_ref, force_ref)
        for block in range(COLUMN):
            span = pl.ds(block * SLOTS, SLOTS)
            grad = grad_ref[0, span, :].astype(F32)
            hidden = hidden_ref[0, span, :].astype(F32)
            for order in range(ORDERS):
                radial = radial_ref[order : order + 1, :]
                place = pl.ds(order * SLOTS, SLOTS)
                left_side[block, place, 0:CHANNELS] = (radial * grad).astype(BF16)
                left_side[block, place, CHANNELS : 2 * CHANNELS] = (radial * hidden).astype(BF16)

    right_side[:, 0:CHANNELS] = near_hidden_ref[0]
    right_side[:, CHANNELS : 2 * CHANNELS] = near_grad_ref[0]
    near_places = [true_rows(near_ref, column, near) for near in range(COLUMN)]
    for block in range(COLUMN):
        pair = dot(left_side[block], right_side[...], ((1,), (1,)))
        for start in range(0, SLOTS, CHUNK):
            span = pl.ds(block * SLOTS + start, CHUNK)
            strength = jnp.zeros((CHUNK, ATOMS), F32)
            for order in range(ORDERS):
                rows = pair[order * SLOTS + start : order * SLOTS + start + CHUNK, :]
                strength = strength + rows * slope_ref[0, order, span, :].astype(F32)
            for axis in range(3):
                total = force_ref[axis, span, :]
                for near in range(COLUMN):
                    row = near_places[near][axis]
                    if axis == 2:
                        row = row + (SIDE / REACH) * offset_z(block, near)
                    part = strength[:, near * SLOTS : (near + 1) * SLOTS]
                    total = total + part * (row - own_cols[axis, span, :])
                force_ref[axis, span, :] = total


def kind_kernel(group, slope_ref, projected_ref, near_ref, *refs):
    before_ref = None if group == 1 else refs[0]
    near_kind_ref, table = refs[-2:]

    @pl.when(pl.program_id(0) == 0)
    def _():
        start_from(before_ref, near_kind_ref)

    add_kinds(place_of(group), slope_ref, projected_ref, near_ref, near_kind_ref, table)


def add_kinds(column, slope_ref, projected_ref, near_ref, near_kind, table):
    projected = projected_ref[0].astype(F32)
    total = near_kind[...]
    for order in range(ORDERS):
        values = [
            projected[order * KINDS : (order + 1) * KINDS, near * SLOTS : (near + 1) * SLOTS]
            for near in range(COLUMN)
        ]
        fill_table(table.at[order], values, near_ref, column)
        total = total + dot(slope_ref[0, order], table[order], ((1,), (1,)))
    near_kind[...] = total


def last_kernel(
    slope_ref, projected_ref, near_ref, before_ref, own_projected_ref, own_ref, force_ref,
    kind_ref, mixed_ref, mass_ref, new_force_ref, new_velocity_ref, own_cols, table, near_kind,
):
    @pl.when(pl.program_id(0) == 0)
    def _():
        spread_own(own_ref, own_cols)
        near_kind[...] = before_ref[...]

    add_kinds(place_of(2), slope_ref, projected_ref, near_ref, near_kind, table)

    @pl.when(pl.program_id(0) == 2)
    def _():
        lanes = lax.broadcasted_iota(jnp.int32, (SLOTS, SLOTS), 1)
        lane_kind = (lanes % KINDS).astype(F32)
        part = lanes // KINDS
        inner = lax.broadcasted_iota(jnp.int32, (ORDERS * KINDS, SLOTS), 0)
        outer = lax.broadcasted_iota(jnp.int32, (ORDERS * KINDS, SLOTS), 1) % KINDS
        slots = lax.broadcasted_iota(jnp.int32, (1, SLOTS), 1)
        for block in range(COLUMN):
            span = pl.ds(block * SLOTS, SLOTS)
            kinds = turned(own_ref[0, block, 3:4, :])
            total = jnp.where(kinds == lane_kind, near_kind[span, :], 0.0)
            own = own_projected_ref[0, :, span]
            for order in range(ORDERS):
                chosen = jnp.where(inner == outer + order * KINDS, 1.0, 0.0).astype(BF16)
                spread = dot(own, chosen, ((0,), (0,)))
                total = total + spread * kind_ref[order, span, :]
            for axis in range(3):
                factor = jnp.zeros((SLOTS, SLOTS), F32)
                for near in range(COLUMN):
                    shift = -own_cols[axis, span, :]
                    if axis == 2:
                        shift = shift + (SIDE / REACH) * offset_z(block, near)
                    factor = jnp.where(part == near, shift, factor)
                here = jnp.logical_or(
                    part == COLUMN + 2 * axis, part == COLUMN + 1 + 2 * axis
                )
                factor = jnp.where(here, 1.0, factor)
                lanes_force = force_ref[axis, span, :] + total * factor
                summed = jnp.sum(lanes_force.T, axis=0, keepdims=True)
                live = slots.astype(F32) < own_ref[0, block, 4:5, :]
                force = jnp.where(live, summed * (2.0 / REACH), 0.0)
                row = 3 * block + axis
                new_force_ref[row] = force
                new_velocity_ref[row] = mixed_ref[row] + HALF_STEP * force / mass_ref[block]


RADIAL_ONE = 0
RADIAL_TWO = ORDERS
TABLE = ORDERS * KINDS
MIX_ONE = CHANNELS
MIX_TWO = 2 * CHANNELS
WIDE = 3 * CHANNELS
UPSTREAM = 2 * ATOMS
WEIGHT_ROWS = 3 * ATOMS


def prepare_kernel(
    counts_ref, masses_ref, positions_ref, velocities_ref, forces_ref, noise_ref, species_ref,
    pair_list_ref, embedding_ref, radial_one_ref, radial_two_ref, mix_one_ref, mix_two_ref,
    readout_ref, new_positions_ref, geometry_ref, mixed_ref, mass_ref, weights_ref,
):
    geometry_ref[...] = jnp.zeros_like(geometry_ref)
    kinds = embedding_ref.shape[0]
    weights_ref[RADIAL_ONE : RADIAL_ONE + ORDERS, :] = radial_one_ref[...]
    weights_ref[RADIAL_TWO : RADIAL_TWO + ORDERS, :] = radial_two_ref[...].astype(F32)
    weights_ref[MIX_ONE : MIX_ONE + CHANNELS, :] = mix_one_ref[...].astype(F32)
    weights_ref[MIX_TWO : MIX_TWO + CHANNELS, :] = mix_two_ref[...].astype(F32)
    weights_ref[WIDE : WIDE + SLOTS, :] = jnp.zeros((SLOTS, CHANNELS), F32)
    weights_ref[WIDE : WIDE + kinds, :] = embedding_ref[...].astype(F32)
    for order in range(ORDERS):
        weights_ref[TABLE + order * KINDS : TABLE + (order + 1) * KINDS, :] = (
            radial_one_ref[order : order + 1, :] * weights_ref[WIDE : WIDE + KINDS, :]
        )
    slots = lax.broadcasted_iota(jnp.int32, (SLOTS, CHANNELS), 0)
    for block in range(COLUMN):
        live = slots < counts_ref[0, 0, block]
        start = UPSTREAM + block * SLOTS
        weights_ref[start : start + SLOTS, :] = jnp.where(live, readout_ref[...], 0.0)
        species = species_ref[block]
        mass = jnp.zeros((1, SLOTS), F32)
        for kind in range(kinds):
            mass = jnp.where(species == kind, masses_ref[kind], mass)
        mass_ref[block] = mass
        for axis in range(3):
            row = 3 * block + axis
            half_velocity = velocities_ref[row] + HALF_STEP * forces_ref[row] / mass
            half_position = positions_ref[row] + HALF_STEP * half_velocity
            mixed = (
                DECAY * half_velocity
                + jnp.sqrt((1.0 - DECAY * DECAY) / mass) * noise_ref[row]
            )
            new_positions = half_position + HALF_STEP * mixed
            mixed_ref[row] = mixed
            new_positions_ref[row] = new_positions
            geometry_ref[block, axis : axis + 1, :] = new_positions
        geometry_ref[block, 3:4, :] = species.astype(F32)
        geometry_ref[block, 4:5, :] = jnp.full(
            (1, SLOTS), counts_ref[0, 0, block], jnp.int32
        ).astype(F32)
        geometry_ref[block, 5:6, 0:13] = pair_list_ref[block].astype(F32)


def shift(cell, axis, step):
    count = lax.axis_size(axis)
    return lax.ppermute(cell, axis, [((i + step) % count, i) for i in range(count)])


def own_row(cell):
    return jnp.stack([shift(cell, "gy", -1), cell, shift(cell, "gy", 1)])


def outer_rows(row):
    return shift(row, "gx", -1), shift(row, "gx", 1)


SMEM = pl.BlockSpec(memory_space=pltpu.SMEM)


def whole(*shape):
    return pl.BlockSpec(
        shape, lambda column: (0,) * len(shape), pipeline_mode=pl.Buffered(1)
    )


def weight(first, rows):
    return pl.BlockSpec(
        (rows, CHANNELS), lambda column: (first // rows, 0), pipeline_mode=pl.Buffered(1)
    )


def result(*shape):
    return pl.BlockSpec(shape, lambda column: (0,) * len(shape))


def at_column(*shape):
    return pl.BlockSpec((1,) + shape, lambda column: (column,) + (0,) * len(shape))


def at_centre(*shape):
    return pl.BlockSpec((1,) + shape, lambda column: (1,) + (0,) * len(shape))


def outer_specs(*shape):
    zeros = (0,) * len(shape)
    return [
        pl.BlockSpec((1,) + shape, lambda column: (jnp.minimum(column, 2),) + zeros),
        pl.BlockSpec((1,) + shape, lambda column: (jnp.maximum(column - 3, 0),) + zeros),
    ]


def call(kernel, name, columns, out_shape, in_specs, out_specs, scratch, flops):
    return pl.pallas_call(
        kernel,
        name=name,
        out_shape=out_shape,
        grid=(columns,),
        in_specs=in_specs,
        out_specs=out_specs,
        scratch_shapes=scratch,
        cost_estimate=pl.CostEstimate(
            flops=columns * flops, bytes_accessed=columns * PAIR_BYTES, transcendentals=0
        ),
        compiler_params=pltpu.CompilerParams(
            dimension_semantics=("arbitrary",), vmem_limit_bytes=LIMIT
        ),
    )


def shape_of(*shape, kind=F32):
    return jax.ShapeDtypeStruct(shape, kind)


PAIR_BYTES = ORDERS * ATOMS * ATOMS * 2
PAIR_FLOPS = ORDERS * ATOMS * ATOMS * CHANNELS * 2


def on_device(
    positions, velocities, forces, noise, species, counts, pair_list, masses, embedding,
    radial_one, mix_one, radial_two, mix_two, readout,
):
    vmem = pl.BlockSpec(memory_space=pltpu.VMEM)
    rows = (3 * COLUMN, 1, SLOTS)
    new_positions, geometry, mixed_velocity, atom_mass, weights = pl.pallas_call(
        prepare_kernel,
        name="prepare",
        out_shape=(
            shape_of(*rows),
            shape_of(COLUMN, 8, SLOTS),
            shape_of(*rows),
            shape_of(COLUMN, 1, SLOTS),
            shape_of(WEIGHT_ROWS, CHANNELS),
        ),
        in_specs=[SMEM, SMEM] + [vmem] * 12,
    )(
        counts, masses, positions.reshape(rows), velocities.reshape(rows), forces.reshape(rows),
        noise.reshape(rows), species.reshape(COLUMN, 1, SLOTS), pair_list.reshape(COLUMN, 1, 13),
        embedding, radial_one, radial_two, mix_one, mix_two, readout[None, :],
    )

    cols = pltpu.VMEM((3, ATOMS, SLOTS), F32)
    place = pltpu.VMEM((1, COLUMN, 8, SLOTS), F32)
    message = pltpu.VMEM((ATOMS, CHANNELS), F32)
    square = pltpu.VMEM((SLOTS, SLOTS), F32)
    flags = [pltpu.VMEM((16, SLOTS), F32), pltpu.VMEM((16, SLOTS), F32)]
    pairs = (ORDERS, ATOMS, ATOMS)
    cell = (COLUMN, 8, SLOTS)
    field = (ATOMS, CHANNELS)
    own_spec = at_centre(*cell)
    radial_one_spec = weight(RADIAL_ONE, ORDERS)
    radial_two_spec = weight(RADIAL_TWO, ORDERS)
    mix_one_spec = weight(MIX_ONE, CHANNELS)
    mix_two_spec = weight(MIX_TWO, CHANNELS)
    wide_spec = weight(WIDE, SLOTS)
    upstream_spec = weight(UPSTREAM, ATOMS)

    geometry_row = own_row(geometry)
    geometry_outer = outer_rows(geometry_row)
    geometries = (geometry_outer[0], geometry_row, geometry_outer[1])
    basis_scratch = [cols, place, square, *flags, message, pltpu.VMEM(field, BF16)]
    basis_row, message_row = call(
        functools.partial(basis_kernel, 1),
        "basis_row",
        3,
        (shape_of(3, *pairs, kind=BF16), shape_of(*field)),
        [own_spec, at_column(*cell), wide_spec, radial_one_spec],
        (at_column(*pairs), result(*field)),
        basis_scratch,
        PAIR_FLOPS,
    )(geometry_row, geometry_row, weights, weights)
    basis_outer, hidden, first_gate = call(
        functools.partial(basis_kernel, OUTER),
        "basis_outer",
        6,
        (shape_of(6, *pairs, kind=BF16), shape_of(*field, kind=BF16), shape_of(*field)),
        [own_spec, *outer_specs(*cell), wide_spec, radial_one_spec, mix_one_spec, whole(*field)],
        (at_column(*pairs), result(*field), result(*field)),
        basis_scratch,
        PAIR_FLOPS,
    )(geometry_row, *geometry_outer, weights, weights, weights, message_row)

    def slope_of(group, before):
        sums = (ORDERS, ATOMS, SLOTS)
        return call(
            functools.partial(slope_kernel, group),
            f"slope_{group}",
            3,
            (shape_of(3, *pairs, kind=BF16), shape_of(*sums)),
            [own_spec, at_column(*cell)] + [whole(*sums)] * len(before),
            (at_column(*pairs), result(*sums)),
            [cols, square, *flags, pltpu.VMEM((SLOTS, ATOMS), BF16)],
            PAIR_FLOPS,
        )(geometry_row, geometries[group], *before)

    def gather_row(name, row):
        return call(
            gather_kernel,
            name,
            3,
            shape_of(*field),
            [at_column(*pairs), at_column(*field), radial_two_spec],
            result(*field),
            [message],
            PAIR_FLOPS,
        )(basis_row, row, weights)

    hidden_row = own_row(hidden)
    slope_1, kind_sums = slope_of(1, ())
    hidden_row, kind_sums = lax.optimization_barrier((hidden_row, kind_sums))
    hidden_outer = outer_rows(hidden_row)
    second_row = gather_row("second_row", hidden_row)
    slope_0, kind_sums = slope_of(0, (kind_sums,))
    second_row, kind_sums = lax.optimization_barrier((second_row, kind_sums))
    message_grad = call(
        second_kernel,
        "second_outer",
        6,
        shape_of(*field, kind=BF16),
        [
            at_column(*pairs), *outer_specs(*field), radial_two_spec, mix_two_spec, upstream_spec,
            whole(*field),
        ],
        result(*field),
        [message],
        PAIR_FLOPS,
    )(basis_outer, *hidden_outer, weights, weights, weights, second_row)

    grad_row = own_row(message_grad)
    slope_2, kind_sums = slope_of(2, (kind_sums,))
    grad_row, kind_sums = lax.optimization_barrier((grad_row, kind_sums))
    slopes = (slope_0, slope_1, slope_2)
    grad_outer = outer_rows(grad_row)
    projected = call(
        first_kernel,
        "first_outer",
        6,
        shape_of(ORDERS * KINDS, ATOMS, kind=BF16),
        [
            at_column(*pairs), *outer_specs(*field), radial_two_spec, mix_one_spec, upstream_spec,
            whole(*field), weight(TABLE, ORDERS * KINDS), whole(*field),
        ],
        result(ORDERS * KINDS, ATOMS),
        [message],
        PAIR_FLOPS,
    )(
        basis_outer, *grad_outer, weights, weights, weights, first_gate, weights,
        gather_row("first_row", grad_row),
    )

    hiddens = (hidden_outer[0], hidden_row, hidden_outer[1])
    grads = (grad_outer[0], grad_row, grad_outer[1])
    forces_so_far = ()
    for group in (1, 0, 2):
        total = call(
            functools.partial(pair_kernel, group),
            f"pair_{group}",
            3,
            shape_of(3, ATOMS, SLOTS),
            [
                own_spec, at_column(*cell), at_column(*pairs), at_column(*field),
                at_column(*field), at_centre(*field), at_centre(*field), radial_two_spec,
            ]
            + [whole(3, ATOMS, SLOTS)] * len(forces_so_far),
            result(3, ATOMS, SLOTS),
            [
                cols, pltpu.VMEM((COLUMN, ORDERS * SLOTS, 2 * CHANNELS), BF16),
                pltpu.VMEM((ATOMS, 2 * CHANNELS), BF16),
            ],
            2 * PAIR_FLOPS,
        )(
            geometry_row, geometries[group], slopes[group], hiddens[group], grads[group],
            hidden_row, grad_row, weights, *forces_so_far,
        )
        forces_so_far = (total,)

    projected_row = own_row(projected)
    projected_outer = outer_rows(projected_row)
    projecteds = (projected_outer[0], projected_row, projected_outer[1])
    kinds = (ORDERS * KINDS, ATOMS)
    tables = pltpu.VMEM((ORDERS, SLOTS, ATOMS), BF16)
    kind_specs = [at_column(*pairs), at_column(*kinds), at_column(*cell)]
    near_kind = ()
    for group in (1, 0):
        near_kind = (
            call(
                functools.partial(kind_kernel, group),
                f"last_{group}",
                3,
                shape_of(ATOMS, SLOTS),
                kind_specs + [whole(ATOMS, SLOTS)] * len(near_kind),
                result(ATOMS, SLOTS),
                [tables],
                PAIR_FLOPS,
            )(slopes[group], projecteds[group], geometries[group], *near_kind),
        )
    new_forces, new_velocities = call(
        last_kernel,
        "last_2",
        3,
        (shape_of(*rows), shape_of(*rows)),
        kind_specs
        + [
            whole(ATOMS, SLOTS), at_centre(*kinds), own_spec, whole(3, ATOMS, SLOTS),
            whole(ORDERS, ATOMS, SLOTS), whole(*rows), whole(COLUMN, 1, SLOTS),
        ],
        (result(*rows), result(*rows)),
        [cols, tables, pltpu.VMEM((ATOMS, SLOTS), F32)],
        PAIR_FLOPS,
    )(
        slopes[2], projecteds[2], geometries[2], *near_kind, projected_row, geometry_row,
        *forces_so_far, kind_sums, mixed_velocity, atom_mass,
    )
    return tuple(
        value.reshape(positions.shape) for value in (new_positions, new_velocities, new_forces)
    )


def solution(mesh):
    split_spec = P("gx", "gy")
    return jax.shard_map(
        on_device,
        mesh=mesh,
        in_specs=(split_spec,) * 7 + (P(),) * 7,
        out_specs=(split_spec,) * 3,
        check_vma=False,
    )
```

```python
import functools
import math

import jax
import jax.numpy as jnp
from jax import lax
from jax.experimental import pallas as pl
from jax.experimental.pallas import tpu as pltpu
from jax.sharding import PartitionSpec as P

SIDE = 10.0
REACH = 5.0
HALF_STEP = 0.25
DECAY = math.exp(-0.5)
FAR = 1.0e4

ORDERS = 8
KINDS = 8
SLOTS = 128
COLUMN = 3
ATOMS = COLUMN * SLOTS
CHANNELS = 128
PARTS = 9
CHUNK = 32
OUTER = -1
LIMIT = 12 * 2**20

F32 = jnp.float32
BF16 = jnp.bfloat16
HIGHEST = lax.Precision.HIGHEST
ODD = (3.14159265160, -5.16771249, 2.55012026, -0.59890223, 0.07772681)
EVEN = (1.0, -4.93480219, 4.05869615, -1.33500654, 0.23347127, -0.02380946)


def fit_terms():
    import numpy as np

    nodes = 0.5 * np.cos(np.pi * (np.arange(400) + 0.5) / 800)
    odd = np.polynomial.polynomial.polyfit(nodes * nodes, np.sin(np.pi * nodes) / nodes, 4)
    even = np.polynomial.polynomial.polyfit(nodes * nodes, np.cos(np.pi * nodes), 4)
    return tuple(float(value) for value in odd), tuple(float(value) for value in even)


ODD, EVEN = fit_terms()


def horner(terms, square):
    total = terms[-1]
    for term in terms[-2::-1]:
        total = total * square + term
    return total


def turned(row):
    return jnp.broadcast_to(row, (SLOTS, SLOTS)).T


def dot(left, right, contract=((1,), (0,)), precision=None):
    return lax.dot_general(
        left, right, (contract, ((), ())), precision=precision, preferred_element_type=F32
    )


def spread_own(own_ref, own_cols):
    for block in range(COLUMN):
        for axis in range(3):
            own_cols[axis, pl.ds(block * SLOTS, SLOTS), :] = turned(
                own_ref[0, block, axis : axis + 1, :] * (1.0 / REACH)
            )


def mark_diagonal(part, diagonal):
    rows = lax.broadcasted_iota(jnp.int32, (SLOTS, SLOTS), 0)
    lanes = lax.broadcasted_iota(jnp.int32, (SLOTS, SLOTS), 1)
    centre = jnp.logical_and(pl.program_id(0) == 1, part == 1)
    hit = jnp.logical_and(rows == lanes, centre)
    diagonal[...] = jnp.where(hit, FAR * FAR, 0.0)


def offset_z(block, near):
    return (near - block + 1) % 3 - 1


def signs_of(part):
    step = pl.program_id(0)
    if part == OUTER:
        return (1 - 2 * (step // 3)).astype(F32), (1 - step % 3).astype(F32)
    return float(1 - part), (1 - step % 3).astype(F32)


def steps_to(near_ref, near, signs):
    return -signs[0] * near_ref[0, near, 6:7, :], -signs[1] * near_ref[0, near, 7:8, :]


def mark_listed(own_ref, near_ref, signs, picked, listed):
    lanes = lax.broadcasted_iota(jnp.int32, (1, SLOTS), 1).astype(F32)
    for block in range(COLUMN):
        for near in range(COLUMN):
            step_x, step_y = steps_to(near_ref, near, signs)
            stencil = 9.0 * step_x + 3.0 * step_y + (13.0 + offset_z(block, near))
            ahead = jnp.where(lanes == stencil - 14.0, own_ref[0, block, 5:6, :], 0.0)
            behind = jnp.where(lanes == 12.0 - stencil, near_ref[0, near, 5:6, :], 0.0)
            own = jnp.where(jnp.logical_and(stencil == 13.0, lanes == 0.0), 1.0, 0.0)
            row = block * COLUMN + near
            picked[row : row + 1, :] = own + ahead + behind
    sums = jnp.sum(picked[...], axis=1, keepdims=True)
    listed[...] = jnp.broadcast_to(sums, listed.shape)


def near_rows(listed, near_ref, signs, block, near):
    x, y, z = true_rows(near_ref, signs, near)
    z = z + (SIDE / REACH) * offset_z(block, near)
    slots = lax.broadcasted_iota(jnp.int32, (1, SLOTS), 1).astype(F32)
    row = block * COLUMN + near
    counts = jnp.logical_and(
        slots < near_ref[0, near, 4:5, :], listed[row : row + 1, :] > 0.5
    )
    return jnp.where(counts, x, FAR), y, z


def left_over(rows, own_cols, diagonal, block, near, start):
    span = pl.ds(block * SLOTS + start, CHUNK)
    dx = rows[0] - own_cols[0, span, :]
    dy = rows[1] - own_cols[1, span, :]
    dz = rows[2] - own_cols[2, span, :]
    square = dx * dx + dy * dy + dz * dz
    if near == block:
        square = square + diagonal[pl.ds(start, CHUNK), :]
    return jnp.maximum(1.0 - square, 0.0)


def species_features(near_ref, embedding, near):
    kinds = turned(near_ref[0, near, 3:4, :])
    lanes = lax.broadcasted_iota(jnp.int32, (SLOTS, SLOTS), 1).astype(F32)
    one_hot = jnp.where(kinds == lanes, 1.0, 0.0).astype(BF16)
    return dot(one_hot, embedding).astype(BF16)


def basis_kernel(part, own_ref, *refs):
    if part == OUTER:
        near_0, near_2, embedding_ref, radial_ref, mix_ref, before_ref = refs[:6]
        basis_ref, hidden_ref, gate_ref = refs[6:9]
        fields = (near_0, near_2)
    else:
        near_1, embedding_ref, radial_ref, basis_ref, after_ref = refs[:5]
        fields = (near_1,)
    own_cols, near_ref, diagonal, picked, listed, message, features = refs[-7:]
    signs = signs_of(part)
    near_ref[0] = pick(fields)

    @pl.when(pl.program_id(0) == 0)
    def _():
        spread_own(own_ref, own_cols)
        picked[...] = jnp.zeros_like(picked)
        if part == OUTER:
            message[...] = before_ref[...]
        else:
            message[...] = jnp.zeros_like(message)

    mark_diagonal(part, diagonal)
    mark_listed(own_ref, near_ref, signs, picked, listed)
    for near in range(COLUMN):
        features[pl.ds(near * SLOTS, SLOTS), :] = species_features(
            near_ref, embedding_ref[...].astype(BF16), near
        )
    for block in range(COLUMN):
        for near in range(COLUMN):
            rows = near_rows(listed, near_ref, signs, block, near)
            for start in range(0, SLOTS, CHUNK):
                left = left_over(rows, own_cols, diagonal, block, near, start)
                middle = left - 0.5
                cosine = middle * horner(ODD, middle * middle)
                twice = cosine + cosine
                last = left * left
                now = last * cosine
                span = (
                    pl.ds(block * SLOTS + start, CHUNK),
                    pl.ds(near * SLOTS, SLOTS),
                )
                basis_ref[0, 0, span[0], span[1]] = last.astype(BF16)
                basis_ref[0, 1, span[0], span[1]] = now.astype(BF16)
                for order in range(2, ORDERS):
                    last, now = now, twice * now - last
                    basis_ref[0, order, span[0], span[1]] = now.astype(BF16)
    gathered = dot(basis_ref[0].reshape(ORDERS * ATOMS, ATOMS), features[...])
    add_orders(gathered, radial_ref, message)

    @pl.when(pl.program_id(0) == pl.num_programs(0) - 1)
    def _():
        if part == OUTER:
            gate = dot(message[...].astype(BF16), mix_ref[...].astype(BF16))
            gate_ref[...] = gate
            base = jnp.concatenate(
                [species_features(own_ref, embedding_ref[...].astype(BF16), block) for block in range(COLUMN)]
            )
            hidden_ref[...] = (base.astype(F32) + gate * jax.nn.sigmoid(gate)).astype(BF16)
        else:
            after_ref[...] = message[...]


def silu_slope(values):
    sigmoid = jax.nn.sigmoid(values)
    return sigmoid * (1.0 + values * (1.0 - sigmoid))


def pick(refs):
    if len(refs) == 1:
        return refs[0][0]
    return jnp.where(pl.program_id(0) < 3, refs[0][0], refs[1][0])


def add_orders(gathered, radial_ref, message):
    total = message[...]
    for order in range(ORDERS):
        rows = gathered[order * ATOMS : (order + 1) * ATOMS, :]
        total = total + radial_ref[order : order + 1, :] * rows
    message[...] = total


def gather_kernel(basis_ref, field_ref, radial_ref, after_ref, message):
    @pl.when(pl.program_id(0) == 0)
    def _():
        message[...] = jnp.zeros_like(message)

    gathered = dot(basis_ref[0].reshape(ORDERS * ATOMS, ATOMS), field_ref[0])
    add_orders(gathered, radial_ref, message)

    @pl.when(pl.program_id(0) == 2)
    def _():
        after_ref[...] = message[...]


def gather_outer(basis_ref, fields, radial_ref, before_ref, message):
    @pl.when(pl.program_id(0) == 0)
    def _():
        message[...] = before_ref[...]

    gathered = dot(basis_ref[0].reshape(ORDERS * ATOMS, ATOMS), pick(fields))
    add_orders(gathered, radial_ref, message)


def second_kernel(
    basis_ref, hidden_0, hidden_2, radial_ref, mix_ref, upstream_ref, before_ref, grad_ref, message
):
    gather_outer(basis_ref, (hidden_0, hidden_2), radial_ref, before_ref, message)

    @pl.when(pl.program_id(0) == 5)
    def _():
        gate = dot(message[...].astype(BF16), mix_ref[...].astype(BF16))
        second = (upstream_ref[...] * silu_slope(gate)).astype(BF16)
        grad_ref[...] = dot(second, mix_ref[...].astype(BF16), ((1,), (1,))).astype(BF16)


def first_kernel(
    basis_ref, grad_0, grad_2, radial_ref, mix_ref, upstream_ref, gate_ref, table_ref, before_ref,
    projected_ref, message,
):
    gather_outer(basis_ref, (grad_0, grad_2), radial_ref, before_ref, message)

    @pl.when(pl.program_id(0) == 5)
    def _():
        hidden_grad = upstream_ref[...] + message[...]
        first = (hidden_grad * silu_slope(gate_ref[...])).astype(BF16)
        message_grad = dot(first, mix_ref[...].astype(BF16), ((1,), (1,)))
        projected_ref[...] = dot(
            table_ref[...], message_grad, ((1,), (1,)), HIGHEST
        ).astype(BF16)


def start_from(before_ref, total_ref):
    if before_ref is None:
        total_ref[...] = jnp.zeros_like(total_ref)
    else:
        total_ref[...] = before_ref[...]


def slope_kernel(
    group, own_ref, near_ref, *refs
):
    before_ref = None if group == 1 else refs[0]
    slope_ref, kind_ref, own_cols, diagonal, picked, listed, table = refs[-7:]
    signs = signs_of(group)

    @pl.when(pl.program_id(0) == 0)
    def _():
        spread_own(own_ref, own_cols)
        picked[...] = jnp.zeros_like(picked)
        start_from(before_ref, kind_ref)

    mark_diagonal(group, diagonal)
    mark_listed(own_ref, near_ref, signs, picked, listed)
    one_hots = [kind_rows(near_ref, near) for near in range(COLUMN)]
    fill_table(table, one_hots, near_ref, signs)
    for block in range(COLUMN):
        for near in range(COLUMN):
            rows = near_rows(listed, near_ref, signs, block, near)
            for start in range(0, SLOTS, CHUNK):
                left = left_over(rows, own_cols, diagonal, block, near, start)
                middle = left - 0.5
                square = middle * middle
                cosine = middle * horner(ODD, square)
                sine = horner(EVEN, square)
                twice = cosine + cosine
                last_a = -2.0 * left
                now_a = last_a * cosine
                now_b = (left * left) * (sine * -math.pi)
                last_b = None
                span = (
                    pl.ds(block * SLOTS + start, CHUNK),
                    pl.ds(near * SLOTS, SLOTS),
                )
                slope_ref[0, 0, span[0], span[1]] = last_a.astype(BF16)
                slope_ref[0, 1, span[0], span[1]] = (now_a + now_b).astype(BF16)
                for order in range(2, ORDERS):
                    last_a, now_a = now_a, twice * now_a - last_a
                    if last_b is None:
                        last_b, now_b = now_b, twice * now_b
                    else:
                        last_b, now_b = now_b, twice * now_b - last_b
                    slope_ref[0, order, span[0], span[1]] = (
                        now_a + float(order) * now_b
                    ).astype(BF16)
    sums = dot(slope_ref[0].reshape(ORDERS * ATOMS, ATOMS), table[...], ((1,), (1,)))
    kind_ref[...] += sums.reshape(ORDERS, ATOMS, SLOTS)


def true_rows(near_ref, signs, near):
    steps = steps_to(near_ref, near, signs)
    x = (near_ref[0, near, 0:1, :] + SIDE * steps[0]) * (1.0 / REACH)
    y = (near_ref[0, near, 1:2, :] + SIDE * steps[1]) * (1.0 / REACH)
    return x, y, near_ref[0, near, 2:3, :] * (1.0 / REACH)


def kind_rows(near_ref, near):
    kinds = lax.broadcasted_iota(jnp.int32, (KINDS, SLOTS), 0).astype(F32)
    return jnp.where(near_ref[0, near, 3:4, :] == kinds, 1.0, 0.0)


def fill_table(table, values, near_ref, signs):
    for near in range(COLUMN):
        zero = jnp.zeros((KINDS, SLOTS), F32)
        pieces = [values[near] if part == near else zero for part in range(COLUMN)]
        for row in true_rows(near_ref, signs, near):
            product = values[near] * row
            high = product.astype(BF16).astype(F32)
            pieces.extend((high, product - high))
        pieces.extend([zero] * (SLOTS // KINDS - PARTS))
        table[:, pl.ds(near * SLOTS, SLOTS)] = jnp.concatenate(pieces, axis=0).astype(BF16)


def pair_kernel(
    group, own_ref, near_ref, slope_ref, near_hidden_ref, near_grad_ref, hidden_ref, grad_ref,
    radial_ref, *refs,
):
    before_ref = None if group == 1 else refs[0]
    force_ref, own_cols, left_side, right_side = refs[-4:]
    signs = signs_of(group)

    @pl.when(pl.program_id(0) == 0)
    def _():
        spread_own(own_ref, own_cols)
        start_from(before_ref, force_ref)
        for block in range(COLUMN):
            span = pl.ds(block * SLOTS, SLOTS)
            grad = grad_ref[0, span, :].astype(F32)
            hidden = hidden_ref[0, span, :].astype(F32)
            for order in range(ORDERS):
                radial = radial_ref[order : order + 1, :]
                place = pl.ds(order * SLOTS, SLOTS)
                left_side[block, place, 0:CHANNELS] = (radial * grad).astype(BF16)
                left_side[block, place, CHANNELS : 2 * CHANNELS] = (radial * hidden).astype(BF16)

    right_side[:, 0:CHANNELS] = near_hidden_ref[0]
    right_side[:, CHANNELS : 2 * CHANNELS] = near_grad_ref[0]
    near_places = [true_rows(near_ref, signs, near) for near in range(COLUMN)]
    for block in range(COLUMN):
        pair = dot(left_side[block], right_side[...], ((1,), (1,)))
        for start in range(0, SLOTS, CHUNK):
            span = pl.ds(block * SLOTS + start, CHUNK)
            strength = jnp.zeros((CHUNK, ATOMS), F32)
            for order in range(ORDERS):
                rows = pair[order * SLOTS + start : order * SLOTS + start + CHUNK, :]
                strength = strength + rows * slope_ref[0, order, span, :].astype(F32)
            for axis in range(3):
                total = force_ref[axis, span, :]
                for near in range(COLUMN):
                    row = near_places[near][axis]
                    if axis == 2:
                        row = row + (SIDE / REACH) * offset_z(block, near)
                    part = strength[:, near * SLOTS : (near + 1) * SLOTS]
                    total = total + part * (row - own_cols[axis, span, :])
                force_ref[axis, span, :] = total


def kind_kernel(group, slope_ref, projected_ref, near_ref, *refs):
    before_ref = None if group == 1 else refs[0]
    near_kind_ref, table = refs[-2:]

    @pl.when(pl.program_id(0) == 0)
    def _():
        start_from(before_ref, near_kind_ref)

    add_kinds(signs_of(group), slope_ref, projected_ref, near_ref, near_kind_ref, table)


def add_kinds(signs, slope_ref, projected_ref, near_ref, near_kind, table):
    projected = projected_ref[0].astype(F32)
    total = near_kind[...]
    for order in range(ORDERS):
        values = [
            projected[order * KINDS : (order + 1) * KINDS, near * SLOTS : (near + 1) * SLOTS]
            for near in range(COLUMN)
        ]
        fill_table(table.at[order], values, near_ref, signs)
        total = total + dot(slope_ref[0, order], table[order], ((1,), (1,)))
    near_kind[...] = total


def last_kernel(
    slope_ref, projected_ref, near_ref, before_ref, own_projected_ref, own_ref, force_ref,
    kind_ref, mixed_ref, mass_ref, new_force_ref, new_velocity_ref, own_cols, table, near_kind,
):
    @pl.when(pl.program_id(0) == 0)
    def _():
        spread_own(own_ref, own_cols)
        near_kind[...] = before_ref[...]

    add_kinds(signs_of(2), slope_ref, projected_ref, near_ref, near_kind, table)

    @pl.when(pl.program_id(0) == 2)
    def _():
        lanes = lax.broadcasted_iota(jnp.int32, (SLOTS, SLOTS), 1)
        lane_kind = (lanes % KINDS).astype(F32)
        part = lanes // KINDS
        inner = lax.broadcasted_iota(jnp.int32, (ORDERS * KINDS, SLOTS), 0)
        outer = lax.broadcasted_iota(jnp.int32, (ORDERS * KINDS, SLOTS), 1) % KINDS
        slots = lax.broadcasted_iota(jnp.int32, (1, SLOTS), 1)
        for block in range(COLUMN):
            span = pl.ds(block * SLOTS, SLOTS)
            kinds = turned(own_ref[0, block, 3:4, :])
            total = jnp.where(kinds == lane_kind, near_kind[span, :], 0.0)
            own = own_projected_ref[0, :, span]
            for order in range(ORDERS):
                chosen = jnp.where(inner == outer + order * KINDS, 1.0, 0.0).astype(BF16)
                spread = dot(own, chosen, ((0,), (0,)))
                total = total + spread * kind_ref[order, span, :]
            for axis in range(3):
                factor = jnp.zeros((SLOTS, SLOTS), F32)
                for near in range(COLUMN):
                    shift = -own_cols[axis, span, :]
                    if axis == 2:
                        shift = shift + (SIDE / REACH) * offset_z(block, near)
                    factor = jnp.where(part == near, shift, factor)
                here = jnp.logical_or(
                    part == COLUMN + 2 * axis, part == COLUMN + 1 + 2 * axis
                )
                factor = jnp.where(here, 1.0, factor)
                lanes_force = force_ref[axis, span, :] + total * factor
                summed = jnp.sum(lanes_force.T, axis=0, keepdims=True)
                live = slots.astype(F32) < own_ref[0, block, 4:5, :]
                force = jnp.where(live, summed * (2.0 / REACH), 0.0)
                row = 3 * block + axis
                new_force_ref[row] = force
                new_velocity_ref[row] = mixed_ref[row] + HALF_STEP * force / mass_ref[block]


RADIAL_ONE = 0
RADIAL_TWO = ORDERS
TABLE = ORDERS * KINDS
MIX_ONE = CHANNELS
MIX_TWO = 2 * CHANNELS
WIDE = 3 * CHANNELS
UPSTREAM = 2 * ATOMS
WEIGHT_ROWS = 3 * ATOMS


def prepare_kernel(
    parity_ref, counts_ref, masses_ref, positions_ref, velocities_ref, forces_ref, noise_ref, species_ref,
    pair_list_ref, embedding_ref, radial_one_ref, radial_two_ref, mix_one_ref, mix_two_ref,
    readout_ref, new_positions_ref, geometry_ref, mixed_ref, mass_ref, weights_ref,
):
    geometry_ref[...] = jnp.zeros_like(geometry_ref)
    kinds = embedding_ref.shape[0]
    weights_ref[RADIAL_ONE : RADIAL_ONE + ORDERS, :] = radial_one_ref[...]
    weights_ref[RADIAL_TWO : RADIAL_TWO + ORDERS, :] = radial_two_ref[...].astype(F32)
    weights_ref[MIX_ONE : MIX_ONE + CHANNELS, :] = mix_one_ref[...].astype(F32)
    weights_ref[MIX_TWO : MIX_TWO + CHANNELS, :] = mix_two_ref[...].astype(F32)
    weights_ref[WIDE : WIDE + SLOTS, :] = jnp.zeros((SLOTS, CHANNELS), F32)
    weights_ref[WIDE : WIDE + kinds, :] = embedding_ref[...].astype(F32)
    for order in range(ORDERS):
        weights_ref[TABLE + order * KINDS : TABLE + (order + 1) * KINDS, :] = (
            radial_one_ref[order : order + 1, :] * weights_ref[WIDE : WIDE + KINDS, :]
        )
    slots = lax.broadcasted_iota(jnp.int32, (SLOTS, CHANNELS), 0)
    for block in range(COLUMN):
        live = slots < counts_ref[0, 0, block]
        start = UPSTREAM + block * SLOTS
        weights_ref[start : start + SLOTS, :] = jnp.where(live, readout_ref[...], 0.0)
        species = species_ref[block]
        mass = jnp.zeros((1, SLOTS), F32)
        for kind in range(kinds):
            mass = jnp.where(species == kind, masses_ref[kind], mass)
        mass_ref[block] = mass
        for axis in range(3):
            row = 3 * block + axis
            half_velocity = velocities_ref[row] + HALF_STEP * forces_ref[row] / mass
            half_position = positions_ref[row] + HALF_STEP * half_velocity
            mixed = (
                DECAY * half_velocity
                + jnp.sqrt((1.0 - DECAY * DECAY) / mass) * noise_ref[row]
            )
            new_positions = half_position + HALF_STEP * mixed
            mixed_ref[row] = mixed
            new_positions_ref[row] = new_positions
            geometry_ref[block, axis : axis + 1, :] = new_positions
        geometry_ref[block, 3:4, :] = species.astype(F32)
        geometry_ref[block, 4:5, :] = jnp.full(
            (1, SLOTS), counts_ref[0, 0, block], jnp.int32
        ).astype(F32)
        for axis in range(2):
            geometry_ref[block, 6 + axis : 7 + axis, :] = jnp.full(
                (1, SLOTS), 1 - 2 * parity_ref[axis], jnp.int32
            ).astype(F32)
        geometry_ref[block, 5:6, 0:13] = pair_list_ref[block].astype(F32)


def swap(cell, axis, first):
    count = lax.axis_size(axis)
    pairs = [((first + i) % count, (first + i + 1) % count) for i in range(0, count, 2)]
    return lax.ppermute(cell, axis, pairs + [(right, left) for left, right in pairs])


def own_row(cell):
    return jnp.stack([swap(cell, "gy", 0), cell, swap(cell, "gy", 1)])


def outer_rows(row):
    return swap(row, "gx", 0), swap(row, "gx", 1)


SMEM = pl.BlockSpec(memory_space=pltpu.SMEM)


def whole(*shape):
    return pl.BlockSpec(
        shape, lambda column: (0,) * len(shape), pipeline_mode=pl.Buffered(1)
    )


def weight(first, rows):
    return pl.BlockSpec(
        (rows, CHANNELS), lambda column: (first // rows, 0), pipeline_mode=pl.Buffered(1)
    )


def result(*shape):
    return pl.BlockSpec(shape, lambda column: (0,) * len(shape))


def at_column(*shape):
    return pl.BlockSpec((1,) + shape, lambda column: (column,) + (0,) * len(shape))


def at_centre(*shape):
    return pl.BlockSpec((1,) + shape, lambda column: (1,) + (0,) * len(shape))


def outer_specs(*shape):
    zeros = (0,) * len(shape)
    return [
        pl.BlockSpec((1,) + shape, lambda column: (jnp.minimum(column, 2),) + zeros),
        pl.BlockSpec((1,) + shape, lambda column: (jnp.maximum(column - 3, 0),) + zeros),
    ]


def call(kernel, name, columns, out_shape, in_specs, out_specs, scratch, flops):
    return pl.pallas_call(
        kernel,
        name=name,
        out_shape=out_shape,
        grid=(columns,),
        in_specs=in_specs,
        out_specs=out_specs,
        scratch_shapes=scratch,
        cost_estimate=pl.CostEstimate(
            flops=columns * flops, bytes_accessed=columns * PAIR_BYTES, transcendentals=0
        ),
        compiler_params=pltpu.CompilerParams(
            dimension_semantics=("arbitrary",), vmem_limit_bytes=LIMIT
        ),
    )


def shape_of(*shape, kind=F32):
    return jax.ShapeDtypeStruct(shape, kind)


PAIR_BYTES = ORDERS * ATOMS * ATOMS * 2
PAIR_FLOPS = ORDERS * ATOMS * ATOMS * CHANNELS * 2


def on_device(
    positions, velocities, forces, noise, species, counts, pair_list, masses, embedding,
    radial_one, mix_one, radial_two, mix_two, readout,
):
    vmem = pl.BlockSpec(memory_space=pltpu.VMEM)
    rows = (3 * COLUMN, 1, SLOTS)
    parity = jnp.stack([lax.axis_index("gx") % 2, lax.axis_index("gy") % 2])
    new_positions, geometry, mixed_velocity, atom_mass, weights = pl.pallas_call(
        prepare_kernel,
        name="prepare",
        out_shape=(
            shape_of(*rows),
            shape_of(COLUMN, 8, SLOTS),
            shape_of(*rows),
            shape_of(COLUMN, 1, SLOTS),
            shape_of(WEIGHT_ROWS, CHANNELS),
        ),
        in_specs=[SMEM] * 3 + [vmem] * 12,
    )(
        parity, counts, masses, positions.reshape(rows), velocities.reshape(rows), forces.reshape(rows),
        noise.reshape(rows), species.reshape(COLUMN, 1, SLOTS), pair_list.reshape(COLUMN, 1, 13),
        embedding, radial_one, radial_two, mix_one, mix_two, readout[None, :],
    )

    cols = pltpu.VMEM((3, ATOMS, SLOTS), F32)
    place = pltpu.VMEM((1, COLUMN, 8, SLOTS), F32)
    message = pltpu.VMEM((ATOMS, CHANNELS), F32)
    square = pltpu.VMEM((SLOTS, SLOTS), F32)
    flags = [pltpu.VMEM((16, SLOTS), F32), pltpu.VMEM((16, SLOTS), F32)]
    pairs = (ORDERS, ATOMS, ATOMS)
    cell = (COLUMN, 8, SLOTS)
    field = (ATOMS, CHANNELS)
    own_spec = at_centre(*cell)
    radial_one_spec = weight(RADIAL_ONE, ORDERS)
    radial_two_spec = weight(RADIAL_TWO, ORDERS)
    mix_one_spec = weight(MIX_ONE, CHANNELS)
    mix_two_spec = weight(MIX_TWO, CHANNELS)
    wide_spec = weight(WIDE, SLOTS)
    upstream_spec = weight(UPSTREAM, ATOMS)

    geometry_row = own_row(geometry)
    geometry_outer = outer_rows(geometry_row)
    geometries = (geometry_outer[0], geometry_row, geometry_outer[1])
    basis_scratch = [cols, place, square, *flags, message, pltpu.VMEM(field, BF16)]
    basis_row, message_row = call(
        functools.partial(basis_kernel, 1),
        "basis_row",
        3,
        (shape_of(3, *pairs, kind=BF16), shape_of(*field)),
        [own_spec, at_column(*cell), wide_spec, radial_one_spec],
        (at_column(*pairs), result(*field)),
        basis_scratch,
        PAIR_FLOPS,
    )(geometry_row, geometry_row, weights, weights)
    basis_outer, hidden, first_gate = call(
        functools.partial(basis_kernel, OUTER),
        "basis_outer",
        6,
        (shape_of(6, *pairs, kind=BF16), shape_of(*field, kind=BF16), shape_of(*field)),
        [own_spec, *outer_specs(*cell), wide_spec, radial_one_spec, mix_one_spec, whole(*field)],
        (at_column(*pairs), result(*field), result(*field)),
        basis_scratch,
        PAIR_FLOPS,
    )(geometry_row, *geometry_outer, weights, weights, weights, message_row)

    def slope_of(group, before):
        sums = (ORDERS, ATOMS, SLOTS)
        return call(
            functools.partial(slope_kernel, group),
            f"slope_{group}",
            3,
            (shape_of(3, *pairs, kind=BF16), shape_of(*sums)),
            [own_spec, at_column(*cell)] + [whole(*sums)] * len(before),
            (at_column(*pairs), result(*sums)),
            [cols, square, *flags, pltpu.VMEM((SLOTS, ATOMS), BF16)],
            PAIR_FLOPS,
        )(geometry_row, geometries[group], *before)

    def gather_row(name, row):
        return call(
            gather_kernel,
            name,
            3,
            shape_of(*field),
            [at_column(*pairs), at_column(*field), radial_two_spec],
            result(*field),
            [message],
            PAIR_FLOPS,
        )(basis_row, row, weights)

    hidden_row = own_row(hidden)
    slope_1, kind_sums = slope_of(1, ())
    hidden_row, kind_sums = lax.optimization_barrier((hidden_row, kind_sums))
    hidden_outer = outer_rows(hidden_row)
    second_row = gather_row("second_row", hidden_row)
    slope_0, kind_sums = slope_of(0, (kind_sums,))
    second_row, kind_sums = lax.optimization_barrier((second_row, kind_sums))
    message_grad = call(
        second_kernel,
        "second_outer",
        6,
        shape_of(*field, kind=BF16),
        [
            at_column(*pairs), *outer_specs(*field), radial_two_spec, mix_two_spec, upstream_spec,
            whole(*field),
        ],
        result(*field),
        [message],
        PAIR_FLOPS,
    )(basis_outer, *hidden_outer, weights, weights, weights, second_row)

    grad_row = own_row(message_grad)
    slope_2, kind_sums = slope_of(2, (kind_sums,))
    grad_row, kind_sums = lax.optimization_barrier((grad_row, kind_sums))
    slopes = (slope_0, slope_1, slope_2)
    grad_outer = outer_rows(grad_row)
    projected = call(
        first_kernel,
        "first_outer",
        6,
        shape_of(ORDERS * KINDS, ATOMS, kind=BF16),
        [
            at_column(*pairs), *outer_specs(*field), radial_two_spec, mix_one_spec, upstream_spec,
            whole(*field), weight(TABLE, ORDERS * KINDS), whole(*field),
        ],
        result(ORDERS * KINDS, ATOMS),
        [message],
        PAIR_FLOPS,
    )(
        basis_outer, *grad_outer, weights, weights, weights, first_gate, weights,
        gather_row("first_row", grad_row),
    )

    hiddens = (hidden_outer[0], hidden_row, hidden_outer[1])
    grads = (grad_outer[0], grad_row, grad_outer[1])
    forces_so_far = ()
    for group in (1, 0, 2):
        total = call(
            functools.partial(pair_kernel, group),
            f"pair_{group}",
            3,
            shape_of(3, ATOMS, SLOTS),
            [
                own_spec, at_column(*cell), at_column(*pairs), at_column(*field),
                at_column(*field), at_centre(*field), at_centre(*field), radial_two_spec,
            ]
            + [whole(3, ATOMS, SLOTS)] * len(forces_so_far),
            result(3, ATOMS, SLOTS),
            [
                cols, pltpu.VMEM((COLUMN, ORDERS * SLOTS, 2 * CHANNELS), BF16),
                pltpu.VMEM((ATOMS, 2 * CHANNELS), BF16),
            ],
            2 * PAIR_FLOPS,
        )(
            geometry_row, geometries[group], slopes[group], hiddens[group], grads[group],
            hidden_row, grad_row, weights, *forces_so_far,
        )
        forces_so_far = (total,)

    projected_row = own_row(projected)
    projected_outer = outer_rows(projected_row)
    projecteds = (projected_outer[0], projected_row, projected_outer[1])
    kinds = (ORDERS * KINDS, ATOMS)
    tables = pltpu.VMEM((ORDERS, SLOTS, ATOMS), BF16)
    kind_specs = [at_column(*pairs), at_column(*kinds), at_column(*cell)]
    near_kind = ()
    for group in (1, 0):
        near_kind = (
            call(
                functools.partial(kind_kernel, group),
                f"last_{group}",
                3,
                shape_of(ATOMS, SLOTS),
                kind_specs + [whole(ATOMS, SLOTS)] * len(near_kind),
                result(ATOMS, SLOTS),
                [tables],
                PAIR_FLOPS,
            )(slopes[group], projecteds[group], geometries[group], *near_kind),
        )
    new_forces, new_velocities = call(
        last_kernel,
        "last_2",
        3,
        (shape_of(*rows), shape_of(*rows)),
        kind_specs
        + [
            whole(ATOMS, SLOTS), at_centre(*kinds), own_spec, whole(3, ATOMS, SLOTS),
            whole(ORDERS, ATOMS, SLOTS), whole(*rows), whole(COLUMN, 1, SLOTS),
        ],
        (result(*rows), result(*rows)),
        [cols, tables, pltpu.VMEM((ATOMS, SLOTS), F32)],
        PAIR_FLOPS,
    )(
        slopes[2], projecteds[2], geometries[2], *near_kind, projected_row, geometry_row,
        *forces_so_far, kind_sums, mixed_velocity, atom_mass,
    )
    return tuple(
        value.reshape(positions.shape) for value in (new_positions, new_velocities, new_forces)
    )


def solution(mesh):
    split_spec = P("gx", "gy")
    return jax.shard_map(
        on_device,
        mesh=mesh,
        in_specs=(split_spec,) * 7 + (P(),) * 7,
        out_specs=(split_spec,) * 3,
        check_vma=False,
    )
```

```python
import functools
import math

import jax
import jax.numpy as jnp
from jax import lax
from jax.experimental import pallas as pl
from jax.experimental.pallas import tpu as pltpu
from jax.sharding import PartitionSpec as P

SIDE = 10.0
REACH = 5.0
HALF_STEP = 0.25
DECAY = math.exp(-0.5)
FAR = 1.0e4

ORDERS = 8
KINDS = 8
SLOTS = 128
COLUMN = 3
ATOMS = COLUMN * SLOTS
CHANNELS = 128
PARTS = 9
CHUNK = 32
OUTER = -1
LIMIT = 8 * 2**20

F32 = jnp.float32
BF16 = jnp.bfloat16
HIGHEST = lax.Precision.HIGHEST
ODD = (3.14159265160, -5.16771249, 2.55012026, -0.59890223, 0.07772681)
EVEN = (1.0, -4.93480219, 4.05869615, -1.33500654, 0.23347127, -0.02380946)


def fit_terms():
    import numpy as np

    nodes = 0.5 * np.cos(np.pi * (np.arange(400) + 0.5) / 800)
    odd = np.polynomial.polynomial.polyfit(nodes * nodes, np.sin(np.pi * nodes) / nodes, 4)
    even = np.polynomial.polynomial.polyfit(nodes * nodes, np.cos(np.pi * nodes), 4)
    return tuple(float(value) for value in odd), tuple(float(value) for value in even)


ODD, EVEN = fit_terms()


def horner(terms, square):
    total = terms[-1]
    for term in terms[-2::-1]:
        total = total * square + term
    return total


def turned(row):
    return jnp.broadcast_to(row, (SLOTS, SLOTS)).T


def dot(left, right, contract=((1,), (0,)), precision=None):
    return lax.dot_general(
        left, right, (contract, ((), ())), precision=precision, preferred_element_type=F32
    )


def spread_own(own_ref, own_cols):
    for block in range(COLUMN):
        for axis in range(3):
            own_cols[axis, pl.ds(block * SLOTS, SLOTS), :] = turned(
                own_ref[0, block, axis : axis + 1, :] * (1.0 / REACH)
            )


def mark_diagonal(part, diagonal):
    rows = lax.broadcasted_iota(jnp.int32, (SLOTS, SLOTS), 0)
    lanes = lax.broadcasted_iota(jnp.int32, (SLOTS, SLOTS), 1)
    centre = jnp.logical_and(pl.program_id(0) == 1, part == 1)
    hit = jnp.logical_and(rows == lanes, centre)
    diagonal[...] = jnp.where(hit, FAR * FAR, 0.0)


def offset_z(block, near):
    return (near - block + 1) % 3 - 1


def signs_of(part):
    step = pl.program_id(0)
    along_x = (1 - step % 3).astype(F32)
    if part == OUTER:
        return along_x, (1 - 2 * (step // 3)).astype(F32)
    return along_x, float(1 - part)


def steps_to(near_ref, near, signs):
    return -signs[0] * near_ref[0, near, 6:7, :], -signs[1] * near_ref[0, near, 7:8, :]


def mark_listed(own_ref, near_ref, signs, picked, listed):
    lanes = lax.broadcasted_iota(jnp.int32, (1, SLOTS), 1).astype(F32)
    for block in range(COLUMN):
        for near in range(COLUMN):
            step_x, step_y = steps_to(near_ref, near, signs)
            stencil = 9.0 * step_x + 3.0 * step_y + (13.0 + offset_z(block, near))
            ahead = jnp.where(lanes == stencil - 14.0, own_ref[0, block, 5:6, :], 0.0)
            behind = jnp.where(lanes == 12.0 - stencil, near_ref[0, near, 5:6, :], 0.0)
            own = jnp.where(jnp.logical_and(stencil == 13.0, lanes == 0.0), 1.0, 0.0)
            row = block * COLUMN + near
            picked[row : row + 1, :] = own + ahead + behind
    sums = jnp.sum(picked[...], axis=1, keepdims=True)
    listed[...] = jnp.broadcast_to(sums, listed.shape)


def near_rows(listed, near_ref, signs, block, near):
    x, y, z = true_rows(near_ref, signs, near)
    z = z + (SIDE / REACH) * offset_z(block, near)
    slots = lax.broadcasted_iota(jnp.int32, (1, SLOTS), 1).astype(F32)
    row = block * COLUMN + near
    counts = jnp.logical_and(
        slots < near_ref[0, near, 4:5, :], listed[row : row + 1, :] > 0.5
    )
    return jnp.where(counts, x, FAR), y, z


def left_over(rows, own_cols, diagonal, block, near, start):
    span = pl.ds(block * SLOTS + start, CHUNK)
    dx = rows[0] - own_cols[0, span, :]
    dy = rows[1] - own_cols[1, span, :]
    dz = rows[2] - own_cols[2, span, :]
    square = dx * dx + dy * dy + dz * dz
    if near == block:
        square = square + diagonal[pl.ds(start, CHUNK), :]
    return jnp.maximum(1.0 - square, 0.0)


def species_features(near_ref, embedding, near):
    kinds = turned(near_ref[0, near, 3:4, :])
    lanes = lax.broadcasted_iota(jnp.int32, (SLOTS, SLOTS), 1).astype(F32)
    one_hot = jnp.where(kinds == lanes, 1.0, 0.0).astype(BF16)
    return dot(one_hot, embedding).astype(BF16)


def basis_kernel(part, own_ref, *refs):
    if part == OUTER:
        near_0, near_2, embedding_ref, radial_ref, mix_ref, before_ref = refs[:6]
        basis_ref, hidden_ref, gate_ref = refs[6:9]
        fields = (near_0, near_2)
    else:
        near_1, embedding_ref, radial_ref, basis_ref, after_ref = refs[:5]
        fields = (near_1,)
    own_cols, near_ref, diagonal, picked, listed, message, features = refs[-7:]
    signs = signs_of(part)
    near_ref[0] = pick(fields)

    @pl.when(pl.program_id(0) == 0)
    def _():
        spread_own(own_ref, own_cols)
        picked[...] = jnp.zeros_like(picked)
        if part == OUTER:
            message[...] = before_ref[...]
        else:
            message[...] = jnp.zeros_like(message)

    mark_diagonal(part, diagonal)
    mark_listed(own_ref, near_ref, signs, picked, listed)
    for near in range(COLUMN):
        features[pl.ds(near * SLOTS, SLOTS), :] = species_features(
            near_ref, embedding_ref[...].astype(BF16), near
        )
    for block in range(COLUMN):
        for near in range(COLUMN):
            rows = near_rows(listed, near_ref, signs, block, near)
            for start in range(0, SLOTS, CHUNK):
                left = left_over(rows, own_cols, diagonal, block, near, start)
                middle = left - 0.5
                cosine = middle * horner(ODD, middle * middle)
                twice = cosine + cosine
                last = left * left
                now = last * cosine
                span = (
                    pl.ds(block * SLOTS + start, CHUNK),
                    pl.ds(near * SLOTS, SLOTS),
                )
                basis_ref[0, 0, span[0], span[1]] = last.astype(BF16)
                basis_ref[0, 1, span[0], span[1]] = now.astype(BF16)
                for order in range(2, ORDERS):
                    last, now = now, twice * now - last
                    basis_ref[0, order, span[0], span[1]] = now.astype(BF16)
    gathered = dot(basis_ref[0].reshape(ORDERS * ATOMS, ATOMS), features[...])
    add_orders(gathered, radial_ref, message)

    @pl.when(pl.program_id(0) == pl.num_programs(0) - 1)
    def _():
        if part == OUTER:
            gate = dot(message[...].astype(BF16), mix_ref[...].astype(BF16))
            gate_ref[...] = gate
            base = jnp.concatenate(
                [species_features(own_ref, embedding_ref[...].astype(BF16), block) for block in range(COLUMN)]
            )
            hidden_ref[...] = (base.astype(F32) + gate * jax.nn.sigmoid(gate)).astype(BF16)
        else:
            after_ref[...] = message[...]


def silu_slope(values):
    sigmoid = jax.nn.sigmoid(values)
    return sigmoid * (1.0 + values * (1.0 - sigmoid))


def pick(refs):
    if len(refs) == 1:
        return refs[0][0]
    return jnp.where(pl.program_id(0) < 3, refs[0][0], refs[1][0])


def add_orders(gathered, radial_ref, message):
    total = message[...]
    for order in range(ORDERS):
        rows = gathered[order * ATOMS : (order + 1) * ATOMS, :]
        total = total + radial_ref[order : order + 1, :] * rows
    message[...] = total


def gather_columns(basis_ref, first, field_ref, radial_ref, message):
    def add(column, carry):
        gathered = dot(
            basis_ref[first + column].reshape(ORDERS * ATOMS, ATOMS), field_ref[column]
        )
        add_orders(gathered, radial_ref, message)
        return carry

    lax.fori_loop(0, 3, add, 0)


def gather_kernel(basis_ref, field_ref, weights_ref, after_ref):
    after_ref[...] = jnp.zeros_like(after_ref)
    radial_ref = rows_of(weights_ref, RADIAL_TWO, ORDERS)
    gather_columns(basis_ref, 0, field_ref, radial_ref, after_ref)


def gather_outer(basis_ref, fields, radial_ref, before_ref, message):
    message[...] = before_ref[...]
    for group, field_ref in enumerate(fields):
        gather_columns(basis_ref, 3 * group, field_ref, radial_ref, message)


def rows_of(weights_ref, first, rows):
    return weights_ref.at[first : first + rows, :]


def second_kernel(basis_ref, hidden_0, hidden_2, weights_ref, before_ref, grad_ref, message):
    radial_ref = rows_of(weights_ref, RADIAL_TWO, ORDERS)
    mix_ref = rows_of(weights_ref, MIX_TWO, CHANNELS)
    upstream_ref = rows_of(weights_ref, UPSTREAM, ATOMS)
    gather_outer(basis_ref, (hidden_0, hidden_2), radial_ref, before_ref, message)
    gate = dot(message[...].astype(BF16), mix_ref[...].astype(BF16))
    second = (upstream_ref[...] * silu_slope(gate)).astype(BF16)
    grad_ref[...] = dot(second, mix_ref[...].astype(BF16), ((1,), (1,))).astype(BF16)


def first_kernel(
    basis_ref, grad_0, grad_2, weights_ref, gate_ref, before_ref, projected_ref, message
):
    radial_ref = rows_of(weights_ref, RADIAL_TWO, ORDERS)
    mix_ref = rows_of(weights_ref, MIX_ONE, CHANNELS)
    upstream_ref = rows_of(weights_ref, UPSTREAM, ATOMS)
    table_ref = rows_of(weights_ref, TABLE, ORDERS * KINDS)
    gather_outer(basis_ref, (grad_0, grad_2), radial_ref, before_ref, message)
    hidden_grad = upstream_ref[...] + message[...]
    first = (hidden_grad * silu_slope(gate_ref[...])).astype(BF16)
    message_grad = dot(first, mix_ref[...].astype(BF16), ((1,), (1,)))
    projected_ref[...] = dot(table_ref[...], message_grad, ((1,), (1,)), HIGHEST).astype(BF16)


def start_from(before_ref, total_ref):
    if before_ref is None:
        total_ref[...] = jnp.zeros_like(total_ref)
    else:
        total_ref[...] = before_ref[...]


def slope_kernel(
    group, own_ref, near_ref, *refs
):
    before_ref = None if group == 1 else refs[0]
    slope_ref, kind_ref, own_cols, diagonal, picked, listed, table = refs[-7:]
    signs = signs_of(group)

    @pl.when(pl.program_id(0) == 0)
    def _():
        spread_own(own_ref, own_cols)
        picked[...] = jnp.zeros_like(picked)
        start_from(before_ref, kind_ref)

    mark_diagonal(group, diagonal)
    mark_listed(own_ref, near_ref, signs, picked, listed)
    one_hots = [kind_rows(near_ref, near) for near in range(COLUMN)]
    fill_table(table, one_hots, near_ref, signs)
    for block in range(COLUMN):
        for near in range(COLUMN):
            rows = near_rows(listed, near_ref, signs, block, near)
            for start in range(0, SLOTS, CHUNK):
                left = left_over(rows, own_cols, diagonal, block, near, start)
                middle = left - 0.5
                square = middle * middle
                cosine = middle * horner(ODD, square)
                sine = horner(EVEN, square)
                twice = cosine + cosine
                last = -2.0 * left
                last_g = (left * left) * (sine * (-2.0 * math.pi))
                now = last * cosine + 0.5 * last_g
                now_g = last_g * cosine
                span = (pl.ds(block * SLOTS + start, CHUNK), pl.ds(near * SLOTS, SLOTS))
                slope_ref[0, 0, span[0], span[1]] = last.astype(BF16)
                slope_ref[0, 1, span[0], span[1]] = now.astype(BF16)
                for order in range(2, ORDERS):
                    last, now = now, twice * now - last + now_g
                    if order < ORDERS - 1:
                        last_g, now_g = now_g, twice * now_g - last_g
                    slope_ref[0, order, span[0], span[1]] = now.astype(BF16)
    sums = dot(slope_ref[0].reshape(ORDERS * ATOMS, ATOMS), table[...], ((1,), (1,)))
    kind_ref[...] += sums.reshape(ORDERS, ATOMS, SLOTS)


def true_rows(near_ref, signs, near):
    steps = steps_to(near_ref, near, signs)
    x = (near_ref[0, near, 0:1, :] + SIDE * steps[0]) * (1.0 / REACH)
    y = (near_ref[0, near, 1:2, :] + SIDE * steps[1]) * (1.0 / REACH)
    return x, y, near_ref[0, near, 2:3, :] * (1.0 / REACH)


def kind_rows(near_ref, near):
    kinds = lax.broadcasted_iota(jnp.int32, (KINDS, SLOTS), 0).astype(F32)
    return jnp.where(near_ref[0, near, 3:4, :] == kinds, 1.0, 0.0)


def fill_table(table, values, near_ref, signs):
    for near in range(COLUMN):
        zero = jnp.zeros((KINDS, SLOTS), F32)
        pieces = [values[near] if part == near else zero for part in range(COLUMN)]
        for row in true_rows(near_ref, signs, near):
            product = values[near] * row
            high = product.astype(BF16).astype(F32)
            pieces.extend((high, product - high))
        pieces.extend([zero] * (SLOTS // KINDS - PARTS))
        table[:, pl.ds(near * SLOTS, SLOTS)] = jnp.concatenate(pieces, axis=0).astype(BF16)


def pair_kernel(
    group, own_ref, near_ref, slope_ref, near_hidden_ref, near_grad_ref, hidden_ref, grad_ref,
    radial_ref, *refs,
):
    before_ref = None if group == 1 else refs[0]
    force_ref, own_cols, left_side, right_side = refs[-4:]
    signs = signs_of(group)

    @pl.when(pl.program_id(0) == 0)
    def _():
        spread_own(own_ref, own_cols)
        start_from(before_ref, force_ref)
        for block in range(COLUMN):
            span = pl.ds(block * SLOTS, SLOTS)
            grad = grad_ref[0, span, :].astype(F32)
            hidden = hidden_ref[0, span, :].astype(F32)
            for order in range(ORDERS):
                radial = radial_ref[order : order + 1, :]
                place = pl.ds(order * SLOTS, SLOTS)
                left_side[block, place, 0:CHANNELS] = (radial * grad).astype(BF16)
                left_side[block, place, CHANNELS : 2 * CHANNELS] = (radial * hidden).astype(BF16)

    right_side[:, 0:CHANNELS] = near_hidden_ref[0]
    right_side[:, CHANNELS : 2 * CHANNELS] = near_grad_ref[0]
    near_places = [true_rows(near_ref, signs, near) for near in range(COLUMN)]
    for block in range(COLUMN):
        pair = dot(left_side[block], right_side[...], ((1,), (1,)))
        for start in range(0, SLOTS, CHUNK):
            span = pl.ds(block * SLOTS + start, CHUNK)
            strength = jnp.zeros((CHUNK, ATOMS), F32)
            for order in range(ORDERS):
                rows = pair[order * SLOTS + start : order * SLOTS + start + CHUNK, :]
                strength = strength + rows * slope_ref[0, order, span, :].astype(F32)
            for axis in range(3):
                total = force_ref[axis, span, :]
                for near in range(COLUMN):
                    row = near_places[near][axis]
                    if axis == 2:
                        row = row + (SIDE / REACH) * offset_z(block, near)
                    part = strength[:, near * SLOTS : (near + 1) * SLOTS]
                    total = total + part * (row - own_cols[axis, span, :])
                force_ref[axis, span, :] = total


def kind_kernel(group, slope_ref, projected_ref, near_ref, *refs):
    before_ref = None if group == 1 else refs[0]
    near_kind_ref, table = refs[-2:]

    @pl.when(pl.program_id(0) == 0)
    def _():
        start_from(before_ref, near_kind_ref)

    add_kinds(signs_of(group), slope_ref, projected_ref, near_ref, near_kind_ref, table)


def add_kinds(signs, slope_ref, projected_ref, near_ref, near_kind, table):
    projected = projected_ref[0].astype(F32)
    total = near_kind[...]
    for order in range(ORDERS):
        values = [
            projected[order * KINDS : (order + 1) * KINDS, near * SLOTS : (near + 1) * SLOTS]
            for near in range(COLUMN)
        ]
        fill_table(table.at[order], values, near_ref, signs)
        total = total + dot(slope_ref[0, order], table[order], ((1,), (1,)))
    near_kind[...] = total


def last_kernel(
    slope_ref, projected_ref, near_ref, before_ref, own_projected_ref, own_ref, force_ref,
    kind_ref, mixed_ref, mass_ref, new_force_ref, new_velocity_ref, own_cols, table, near_kind,
):
    @pl.when(pl.program_id(0) == 0)
    def _():
        spread_own(own_ref, own_cols)
        near_kind[...] = before_ref[...]

    add_kinds(signs_of(2), slope_ref, projected_ref, near_ref, near_kind, table)

    @pl.when(pl.program_id(0) == 2)
    def _():
        lanes = lax.broadcasted_iota(jnp.int32, (SLOTS, SLOTS), 1)
        lane_kind = (lanes % KINDS).astype(F32)
        part = lanes // KINDS
        inner = lax.broadcasted_iota(jnp.int32, (ORDERS * KINDS, SLOTS), 0)
        outer = lax.broadcasted_iota(jnp.int32, (ORDERS * KINDS, SLOTS), 1) % KINDS
        slots = lax.broadcasted_iota(jnp.int32, (1, SLOTS), 1)
        for block in range(COLUMN):
            span = pl.ds(block * SLOTS, SLOTS)
            kinds = turned(own_ref[0, block, 3:4, :])
            total = jnp.where(kinds == lane_kind, near_kind[span, :], 0.0)
            own = own_projected_ref[0, :, span]
            for order in range(ORDERS):
                chosen = jnp.where(inner == outer + order * KINDS, 1.0, 0.0).astype(BF16)
                spread = dot(own, chosen, ((0,), (0,)))
                total = total + spread * kind_ref[order, span, :]
            for axis in range(3):
                factor = jnp.zeros((SLOTS, SLOTS), F32)
                for near in range(COLUMN):
                    shift = -own_cols[axis, span, :]
                    if axis == 2:
                        shift = shift + (SIDE / REACH) * offset_z(block, near)
                    factor = jnp.where(part == near, shift, factor)
                here = jnp.logical_or(
                    part == COLUMN + 2 * axis, part == COLUMN + 1 + 2 * axis
                )
                factor = jnp.where(here, 1.0, factor)
                lanes_force = force_ref[axis, span, :] + total * factor
                summed = jnp.sum(lanes_force.T, axis=0, keepdims=True)
                live = slots.astype(F32) < own_ref[0, block, 4:5, :]
                force = jnp.where(live, summed * (2.0 / REACH), 0.0)
                row = 3 * block + axis
                new_force_ref[row] = force
                new_velocity_ref[row] = mixed_ref[row] + HALF_STEP * force / mass_ref[block]


RADIAL_ONE = 0
RADIAL_TWO = ORDERS
TABLE = ORDERS * KINDS
MIX_ONE = CHANNELS
MIX_TWO = 2 * CHANNELS
WIDE = 3 * CHANNELS
UPSTREAM = 2 * ATOMS
WEIGHT_ROWS = 3 * ATOMS


def prepare_kernel(
    parity_ref, counts_ref, masses_ref, positions_ref, velocities_ref, forces_ref, noise_ref, species_ref,
    pair_list_ref, embedding_ref, radial_one_ref, radial_two_ref, mix_one_ref, mix_two_ref,
    readout_ref, new_positions_ref, geometry_ref, mixed_ref, mass_ref, weights_ref,
):
    geometry_ref[...] = jnp.zeros_like(geometry_ref)
    kinds = embedding_ref.shape[0]
    weights_ref[RADIAL_ONE : RADIAL_ONE + ORDERS, :] = radial_one_ref[...]
    weights_ref[RADIAL_TWO : RADIAL_TWO + ORDERS, :] = radial_two_ref[...].astype(F32)
    weights_ref[MIX_ONE : MIX_ONE + CHANNELS, :] = mix_one_ref[...].astype(F32)
    weights_ref[MIX_TWO : MIX_TWO + CHANNELS, :] = mix_two_ref[...].astype(F32)
    weights_ref[WIDE : WIDE + SLOTS, :] = jnp.zeros((SLOTS, CHANNELS), F32)
    weights_ref[WIDE : WIDE + kinds, :] = embedding_ref[...].astype(F32)
    for order in range(ORDERS):
        weights_ref[TABLE + order * KINDS : TABLE + (order + 1) * KINDS, :] = (
            radial_one_ref[order : order + 1, :] * weights_ref[WIDE : WIDE + KINDS, :]
        )
    slots = lax.broadcasted_iota(jnp.int32, (SLOTS, CHANNELS), 0)
    for block in range(COLUMN):
        live = slots < counts_ref[0, 0, block]
        start = UPSTREAM + block * SLOTS
        weights_ref[start : start + SLOTS, :] = jnp.where(live, readout_ref[...], 0.0)
        species = species_ref[block]
        mass = jnp.zeros((1, SLOTS), F32)
        for kind in range(kinds):
            mass = jnp.where(species == kind, masses_ref[kind], mass)
        mass_ref[block] = mass
        for axis in range(3):
            row = 3 * block + axis
            half_velocity = velocities_ref[row] + HALF_STEP * forces_ref[row] / mass
            half_position = positions_ref[row] + HALF_STEP * half_velocity
            mixed = (
                DECAY * half_velocity
                + jnp.sqrt((1.0 - DECAY * DECAY) / mass) * noise_ref[row]
            )
            new_positions = half_position + HALF_STEP * mixed
            mixed_ref[row] = mixed
            new_positions_ref[row] = new_positions
            geometry_ref[block, axis : axis + 1, :] = new_positions
        geometry_ref[block, 3:4, :] = species.astype(F32)
        geometry_ref[block, 4:5, :] = jnp.full(
            (1, SLOTS), counts_ref[0, 0, block], jnp.int32
        ).astype(F32)
        for axis in range(2):
            geometry_ref[block, 6 + axis : 7 + axis, :] = jnp.full(
                (1, SLOTS), 1 - 2 * parity_ref[axis], jnp.int32
            ).astype(F32)
        geometry_ref[block, 5:6, 0:13] = pair_list_ref[block].astype(F32)


def swap(cell, axis, first):
    count = lax.axis_size(axis)
    pairs = [((first + i) % count, (first + i + 1) % count) for i in range(0, count, 2)]
    return lax.ppermute(cell, axis, pairs + [(right, left) for left, right in pairs])


def own_row(cell):
    return jnp.stack([swap(cell, "gx", 0), cell, swap(cell, "gx", 1)])


def outer_rows(row):
    return swap(row, "gy", 0), swap(row, "gy", 1)


SMEM = pl.BlockSpec(memory_space=pltpu.SMEM)


def whole(*shape):
    return pl.BlockSpec(
        shape, lambda column: (0,) * len(shape), pipeline_mode=pl.Buffered(1)
    )


def weight(first, rows):
    return pl.BlockSpec(
        (rows, CHANNELS), lambda column: (first // rows, 0), pipeline_mode=pl.Buffered(1)
    )


def result(*shape):
    return pl.BlockSpec(shape, lambda column: (0,) * len(shape))


def at_column(*shape):
    return pl.BlockSpec((1,) + shape, lambda column: (column,) + (0,) * len(shape))


def at_centre(*shape):
    return pl.BlockSpec((1,) + shape, lambda column: (1,) + (0,) * len(shape))


def outer_specs(*shape):
    zeros = (0,) * len(shape)
    return [
        pl.BlockSpec((1,) + shape, lambda column: (jnp.minimum(column, 2),) + zeros),
        pl.BlockSpec((1,) + shape, lambda column: (jnp.maximum(column - 3, 0),) + zeros),
    ]


def call(kernel, name, columns, out_shape, in_specs, out_specs, scratch, flops):
    return pl.pallas_call(
        kernel,
        name=name,
        out_shape=out_shape,
        grid=(columns,),
        in_specs=in_specs,
        out_specs=out_specs,
        scratch_shapes=scratch,
        cost_estimate=pl.CostEstimate(
            flops=columns * flops, bytes_accessed=columns * PAIR_BYTES, transcendentals=0
        ),
        compiler_params=pltpu.CompilerParams(
            dimension_semantics=("arbitrary",), vmem_limit_bytes=LIMIT
        ),
    )


def shape_of(*shape, kind=F32):
    return jax.ShapeDtypeStruct(shape, kind)


PAIR_BYTES = ORDERS * ATOMS * ATOMS * 2
PAIR_FLOPS = ORDERS * ATOMS * ATOMS * CHANNELS * 2


def on_device(
    positions, velocities, forces, noise, species, counts, pair_list, masses, embedding,
    radial_one, mix_one, radial_two, mix_two, readout,
):
    vmem = pl.BlockSpec(memory_space=pltpu.VMEM)
    rows = (3 * COLUMN, 1, SLOTS)
    parity = jnp.stack([lax.axis_index("gx") % 2, lax.axis_index("gy") % 2])
    new_positions, geometry, mixed_velocity, atom_mass, weights = pl.pallas_call(
        prepare_kernel,
        name="prepare",
        out_shape=(
            shape_of(*rows),
            shape_of(COLUMN, 8, SLOTS),
            shape_of(*rows),
            shape_of(COLUMN, 1, SLOTS),
            shape_of(WEIGHT_ROWS, CHANNELS),
        ),
        in_specs=[SMEM] * 3 + [vmem] * 12,
    )(
        parity, counts, masses, positions.reshape(rows), velocities.reshape(rows), forces.reshape(rows),
        noise.reshape(rows), species.reshape(COLUMN, 1, SLOTS), pair_list.reshape(COLUMN, 1, 13),
        embedding, radial_one, radial_two, mix_one, mix_two, readout[None, :],
    )

    cols = pltpu.VMEM((3, ATOMS, SLOTS), F32)
    place = pltpu.VMEM((1, COLUMN, 8, SLOTS), F32)
    message = pltpu.VMEM((ATOMS, CHANNELS), F32)
    square = pltpu.VMEM((SLOTS, SLOTS), F32)
    flags = [pltpu.VMEM((16, SLOTS), F32), pltpu.VMEM((16, SLOTS), F32)]
    pairs = (ORDERS, ATOMS, ATOMS)
    cell = (COLUMN, 8, SLOTS)
    field = (ATOMS, CHANNELS)
    own_spec = at_centre(*cell)
    radial_one_spec = weight(RADIAL_ONE, ORDERS)
    radial_two_spec = weight(RADIAL_TWO, ORDERS)
    mix_one_spec = weight(MIX_ONE, CHANNELS)
    mix_two_spec = weight(MIX_TWO, CHANNELS)
    wide_spec = weight(WIDE, SLOTS)
    upstream_spec = weight(UPSTREAM, ATOMS)

    geometry_row = own_row(geometry)
    geometry_outer = outer_rows(geometry_row)
    geometries = (geometry_outer[0], geometry_row, geometry_outer[1])
    basis_scratch = [cols, place, square, *flags, message, pltpu.VMEM(field, BF16)]
    basis_row, message_row = call(
        functools.partial(basis_kernel, 1),
        "basis_row",
        3,
        (shape_of(3, *pairs, kind=BF16), shape_of(*field)),
        [own_spec, at_column(*cell), wide_spec, radial_one_spec],
        (at_column(*pairs), result(*field)),
        basis_scratch,
        PAIR_FLOPS,
    )(geometry_row, geometry_row, weights, weights)
    basis_outer, hidden, first_gate = call(
        functools.partial(basis_kernel, OUTER),
        "basis_outer",
        6,
        (shape_of(6, *pairs, kind=BF16), shape_of(*field, kind=BF16), shape_of(*field)),
        [own_spec, *outer_specs(*cell), wide_spec, radial_one_spec, mix_one_spec, whole(*field)],
        (at_column(*pairs), result(*field), result(*field)),
        basis_scratch,
        PAIR_FLOPS,
    )(geometry_row, *geometry_outer, weights, weights, weights, message_row)

    def slope_of(group, before):
        sums = (ORDERS, ATOMS, SLOTS)
        return call(
            functools.partial(slope_kernel, group),
            f"slope_{group}",
            3,
            (shape_of(3, *pairs, kind=BF16), shape_of(*sums)),
            [own_spec, at_column(*cell)] + [whole(*sums)] * len(before),
            (at_column(*pairs), result(*sums)),
            [cols, square, *flags, pltpu.VMEM((SLOTS, ATOMS), BF16)],
            PAIR_FLOPS,
        )(geometry_row, geometries[group], *before)

    def single(kernel, name, out_shape, scratch, *operands):
        return pl.pallas_call(
            kernel,
            name=name,
            out_shape=out_shape,
            in_specs=[vmem] * len(operands),
            out_specs=vmem,
            scratch_shapes=scratch,
            cost_estimate=pl.CostEstimate(
                flops=6 * PAIR_FLOPS, bytes_accessed=6 * PAIR_BYTES, transcendentals=0
            ),
            compiler_params=pltpu.CompilerParams(vmem_limit_bytes=LIMIT),
        )(*operands)

    def gather_row(name, row):
        return single(gather_kernel, name, shape_of(*field), [], basis_row, row, weights)

    hidden_row = own_row(hidden)
    slope_1, kind_sums = slope_of(1, ())
    hidden_row, kind_sums = lax.optimization_barrier((hidden_row, kind_sums))
    hidden_outer = outer_rows(hidden_row)
    second_row = gather_row("second_row", hidden_row)
    slope_0, kind_sums = slope_of(0, (kind_sums,))
    second_row, kind_sums = lax.optimization_barrier((second_row, kind_sums))
    message_grad = single(
        second_kernel, "second_outer", shape_of(*field, kind=BF16), [message],
        basis_outer, *hidden_outer, weights, second_row,
    )

    grad_row = own_row(message_grad)
    slope_2, kind_sums = slope_of(2, (kind_sums,))
    grad_row, kind_sums = lax.optimization_barrier((grad_row, kind_sums))
    slopes = (slope_0, slope_1, slope_2)
    grad_outer = outer_rows(grad_row)
    projected = single(
        first_kernel, "first_outer", shape_of(ORDERS * KINDS, ATOMS, kind=BF16), [message],
        basis_outer, *grad_outer, weights, first_gate, gather_row("first_row", grad_row),
    )

    hiddens = (hidden_outer[0], hidden_row, hidden_outer[1])
    grads = (grad_outer[0], grad_row, grad_outer[1])
    forces_so_far = ()
    for group in (1, 0, 2):
        total = call(
            functools.partial(pair_kernel, group),
            f"pair_{group}",
            3,
            shape_of(3, ATOMS, SLOTS),
            [
                own_spec, at_column(*cell), at_column(*pairs), at_column(*field),
                at_column(*field), at_centre(*field), at_centre(*field), radial_two_spec,
            ]
            + [whole(3, ATOMS, SLOTS)] * len(forces_so_far),
            result(3, ATOMS, SLOTS),
            [
                cols, pltpu.VMEM((COLUMN, ORDERS * SLOTS, 2 * CHANNELS), BF16),
                pltpu.VMEM((ATOMS, 2 * CHANNELS), BF16),
            ],
            2 * PAIR_FLOPS,
        )(
            geometry_row, geometries[group], slopes[group], hiddens[group], grads[group],
            hidden_row, grad_row, weights, *forces_so_far,
        )
        forces_so_far = (total,)

    projected_row = own_row(projected)
    projected_outer = outer_rows(projected_row)
    projecteds = (projected_outer[0], projected_row, projected_outer[1])
    kinds = (ORDERS * KINDS, ATOMS)
    tables = pltpu.VMEM((ORDERS, SLOTS, ATOMS), BF16)
    kind_specs = [at_column(*pairs), at_column(*kinds), at_column(*cell)]
    near_kind = ()
    for group in (1, 0):
        near_kind = (
            call(
                functools.partial(kind_kernel, group),
                f"last_{group}",
                3,
                shape_of(ATOMS, SLOTS),
                kind_specs + [whole(ATOMS, SLOTS)] * len(near_kind),
                result(ATOMS, SLOTS),
                [tables],
                PAIR_FLOPS,
            )(slopes[group], projecteds[group], geometries[group], *near_kind),
        )
    new_forces, new_velocities = call(
        last_kernel,
        "last_2",
        3,
        (shape_of(*rows), shape_of(*rows)),
        kind_specs
        + [
            whole(ATOMS, SLOTS), at_centre(*kinds), own_spec, whole(3, ATOMS, SLOTS),
            whole(ORDERS, ATOMS, SLOTS), whole(*rows), whole(COLUMN, 1, SLOTS),
        ],
        (result(*rows), result(*rows)),
        [cols, tables, pltpu.VMEM((ATOMS, SLOTS), F32)],
        PAIR_FLOPS,
    )(
        slopes[2], projecteds[2], geometries[2], *near_kind, projected_row, geometry_row,
        *forces_so_far, kind_sums, mixed_velocity, atom_mass,
    )
    return tuple(
        value.reshape(positions.shape) for value in (new_positions, new_velocities, new_forces)
    )


def solution(mesh):
    split_spec = P("gx", "gy")
    return jax.shard_map(
        on_device,
        mesh=mesh,
        in_specs=(split_spec,) * 7 + (P(),) * 7,
        out_specs=(split_spec,) * 3,
        check_vma=False,
    )
```

```python
import functools
import math

import jax
import jax.numpy as jnp
from jax import lax
from jax.experimental import pallas as pl
from jax.experimental.pallas import tpu as pltpu
from jax.sharding import PartitionSpec as P

SIDE = 10.0
REACH = 5.0
HALF_STEP = 0.25
DECAY = math.exp(-0.5)
FAR = 1.0e4

ORDERS = 8
KINDS = 8
SLOTS = 128
COLUMN = 3
ATOMS = COLUMN * SLOTS
CHANNELS = 128
PARTS = 9
CHUNK = 16
OUTER = -1
LIMIT = 8 * 2**20

F32 = jnp.float32
BF16 = jnp.bfloat16
HIGHEST = lax.Precision.HIGHEST
ODD = (3.14159265160, -5.16771249, 2.55012026, -0.59890223, 0.07772681)
EVEN = (1.0, -4.93480219, 4.05869615, -1.33500654, 0.23347127, -0.02380946)


def fit_terms():
    import numpy as np

    nodes = 0.5 * np.cos(np.pi * (np.arange(400) + 0.5) / 800)
    odd = np.polynomial.polynomial.polyfit(nodes * nodes, np.sin(np.pi * nodes) / nodes, 4)
    even = np.polynomial.polynomial.polyfit(nodes * nodes, np.cos(np.pi * nodes), 4)
    return tuple(float(value) for value in odd), tuple(float(value) for value in even)


ODD, EVEN = fit_terms()


def horner(terms, square):
    total = terms[-1]
    for term in terms[-2::-1]:
        total = total * square + term
    return total


def turned(row):
    return jnp.broadcast_to(row, (SLOTS, SLOTS)).T


def dot(left, right, contract=((1,), (0,)), precision=None):
    return lax.dot_general(
        left, right, (contract, ((), ())), precision=precision, preferred_element_type=F32
    )


def spread_own(own_ref, own_cols):
    for block in range(COLUMN):
        for axis in range(3):
            own_cols[axis, pl.ds(block * SLOTS, SLOTS), :] = turned(
                own_ref[0, block, axis : axis + 1, :] * (1.0 / REACH)
            )


def mark_diagonal(part, diagonal):
    rows = lax.broadcasted_iota(jnp.int32, (SLOTS, SLOTS), 0)
    lanes = lax.broadcasted_iota(jnp.int32, (SLOTS, SLOTS), 1)
    centre = jnp.logical_and(pl.program_id(0) == 1, part == 1)
    hit = jnp.logical_and(rows == lanes, centre)
    diagonal[...] = jnp.where(hit, FAR * FAR, 0.0)


def offset_z(block, near):
    return (near - block + 1) % 3 - 1


def signs_of(part):
    step = pl.program_id(0)
    along_x = (1 - step % 3).astype(F32)
    if part == OUTER:
        return along_x, (1 - 2 * (step // 3)).astype(F32)
    return along_x, float(1 - part)


def steps_to(near_ref, near, signs):
    return -signs[0] * near_ref[0, near, 6:7, :], -signs[1] * near_ref[0, near, 7:8, :]


def mark_listed(own_ref, near_ref, signs, picked, listed):
    lanes = lax.broadcasted_iota(jnp.int32, (1, SLOTS), 1).astype(F32)
    for block in range(COLUMN):
        for near in range(COLUMN):
            step_x, step_y = steps_to(near_ref, near, signs)
            stencil = 9.0 * step_x + 3.0 * step_y + (13.0 + offset_z(block, near))
            ahead = jnp.where(lanes == stencil - 14.0, own_ref[0, block, 5:6, :], 0.0)
            behind = jnp.where(lanes == 12.0 - stencil, near_ref[0, near, 5:6, :], 0.0)
            own = jnp.where(jnp.logical_and(stencil == 13.0, lanes == 0.0), 1.0, 0.0)
            row = block * COLUMN + near
            picked[row : row + 1, :] = own + ahead + behind
    sums = jnp.sum(picked[...], axis=1, keepdims=True)
    listed[...] = jnp.broadcast_to(sums, listed.shape)


def near_rows(listed, near_ref, signs, block, near):
    x, y, z = true_rows(near_ref, signs, near)
    z = z + (SIDE / REACH) * offset_z(block, near)
    slots = lax.broadcasted_iota(jnp.int32, (1, SLOTS), 1).astype(F32)
    row = block * COLUMN + near
    counts = jnp.logical_and(
        slots < near_ref[0, near, 4:5, :], listed[row : row + 1, :] > 0.5
    )
    return jnp.where(counts, x, FAR), y, z


def left_over(rows, own_cols, diagonal, block, near, start):
    span = pl.ds(block * SLOTS + start, CHUNK)
    dx = rows[0] - own_cols[0, span, :]
    dy = rows[1] - own_cols[1, span, :]
    dz = rows[2] - own_cols[2, span, :]
    square = dx * dx + dy * dy + dz * dz
    if near == block:
        square = square + diagonal[pl.ds(start, CHUNK), :]
    return jnp.maximum(1.0 - square, 0.0)


def species_features(near_ref, embedding, near):
    kinds = turned(near_ref[0, near, 3:4, :])
    lanes = lax.broadcasted_iota(jnp.int32, (SLOTS, SLOTS), 1).astype(F32)
    one_hot = jnp.where(kinds == lanes, 1.0, 0.0).astype(BF16)
    return dot(one_hot, embedding).astype(BF16)


def basis_kernel(part, own_ref, *refs):
    if part == OUTER:
        near_0, near_2, embedding_ref, radial_ref, mix_ref, before_ref = refs[:6]
        basis_ref, hidden_ref, gate_ref = refs[6:9]
        fields = (near_0, near_2)
    else:
        near_1, embedding_ref, radial_ref, basis_ref, after_ref = refs[:5]
        fields = (near_1,)
    own_cols, near_ref, diagonal, picked, listed, message, features = refs[-7:]
    signs = signs_of(part)
    near_ref[0] = pick(fields)

    @pl.when(pl.program_id(0) == 0)
    def _():
        spread_own(own_ref, own_cols)
        picked[...] = jnp.zeros_like(picked)
        if part == OUTER:
            message[...] = before_ref[...]
        else:
            message[...] = jnp.zeros_like(message)

    mark_diagonal(part, diagonal)
    mark_listed(own_ref, near_ref, signs, picked, listed)
    for near in range(COLUMN):
        features[pl.ds(near * SLOTS, SLOTS), :] = species_features(
            near_ref, embedding_ref[...].astype(BF16), near
        )
    for block in range(COLUMN):
        for near in range(COLUMN):
            rows = near_rows(listed, near_ref, signs, block, near)
            for start in range(0, SLOTS, CHUNK):
                left = left_over(rows, own_cols, diagonal, block, near, start)
                middle = left - 0.5
                cosine = middle * horner(ODD, middle * middle)
                twice = cosine + cosine
                last = left * left
                now = last * cosine
                span = (
                    pl.ds(block * SLOTS + start, CHUNK),
                    pl.ds(near * SLOTS, SLOTS),
                )
                basis_ref[0, 0, span[0], span[1]] = last.astype(BF16)
                basis_ref[0, 1, span[0], span[1]] = now.astype(BF16)
                for order in range(2, ORDERS):
                    last, now = now, twice * now - last
                    basis_ref[0, order, span[0], span[1]] = now.astype(BF16)
    gathered = dot(basis_ref[0].reshape(ORDERS * ATOMS, ATOMS), features[...])
    add_orders(gathered, radial_ref, message)

    @pl.when(pl.program_id(0) == pl.num_programs(0) - 1)
    def _():
        if part == OUTER:
            gate = dot(message[...].astype(BF16), mix_ref[...].astype(BF16))
            gate_ref[...] = gate
            base = jnp.concatenate(
                [species_features(own_ref, embedding_ref[...].astype(BF16), block) for block in range(COLUMN)]
            )
            hidden_ref[...] = (base.astype(F32) + gate * jax.nn.sigmoid(gate)).astype(BF16)
        else:
            after_ref[...] = message[...]


def silu_slope(values):
    sigmoid = jax.nn.sigmoid(values)
    return sigmoid * (1.0 + values * (1.0 - sigmoid))


def pick(refs):
    if len(refs) == 1:
        return refs[0][0]
    return jnp.where(pl.program_id(0) < 3, refs[0][0], refs[1][0])


def add_orders(gathered, radial_ref, message):
    total = message[...]
    for order in range(ORDERS):
        rows = gathered[order * ATOMS : (order + 1) * ATOMS, :]
        total = total + radial_ref[order : order + 1, :] * rows
    message[...] = total


def gather_columns(basis_ref, first, field_ref, radial_ref, message):
    def add(column, carry):
        gathered = dot(
            basis_ref[first + column].reshape(ORDERS * ATOMS, ATOMS), field_ref[column]
        )
        add_orders(gathered, radial_ref, message)
        return carry

    lax.fori_loop(0, 3, add, 0)


def gather_kernel(basis_ref, field_ref, weights_ref, after_ref):
    after_ref[...] = jnp.zeros_like(after_ref)
    radial_ref = rows_of(weights_ref, RADIAL_TWO, ORDERS)
    gather_columns(basis_ref, 0, field_ref, radial_ref, after_ref)


def gather_outer(basis_ref, fields, radial_ref, before_ref, message):
    message[...] = before_ref[...]
    for group, field_ref in enumerate(fields):
        gather_columns(basis_ref, 3 * group, field_ref, radial_ref, message)


def rows_of(weights_ref, first, rows):
    return weights_ref.at[first : first + rows, :]


def second_kernel(basis_ref, hidden_0, hidden_2, weights_ref, before_ref, grad_ref, message):
    radial_ref = rows_of(weights_ref, RADIAL_TWO, ORDERS)
    mix_ref = rows_of(weights_ref, MIX_TWO, CHANNELS)
    upstream_ref = rows_of(weights_ref, UPSTREAM, ATOMS)
    gather_outer(basis_ref, (hidden_0, hidden_2), radial_ref, before_ref, message)
    gate = dot(message[...].astype(BF16), mix_ref[...].astype(BF16))
    second = (upstream_ref[...] * silu_slope(gate)).astype(BF16)
    grad_ref[...] = dot(second, mix_ref[...].astype(BF16), ((1,), (1,))).astype(BF16)


def first_kernel(
    basis_ref, grad_0, grad_2, weights_ref, gate_ref, before_ref, projected_ref, message
):
    radial_ref = rows_of(weights_ref, RADIAL_TWO, ORDERS)
    mix_ref = rows_of(weights_ref, MIX_ONE, CHANNELS)
    upstream_ref = rows_of(weights_ref, UPSTREAM, ATOMS)
    table_ref = rows_of(weights_ref, TABLE, ORDERS * KINDS)
    gather_outer(basis_ref, (grad_0, grad_2), radial_ref, before_ref, message)
    hidden_grad = upstream_ref[...] + message[...]
    first = (hidden_grad * silu_slope(gate_ref[...])).astype(BF16)
    message_grad = dot(first, mix_ref[...].astype(BF16), ((1,), (1,)))
    projected_ref[...] = dot(table_ref[...], message_grad, ((1,), (1,)), HIGHEST).astype(BF16)


def start_from(before_ref, total_ref):
    if before_ref is None:
        total_ref[...] = jnp.zeros_like(total_ref)
    else:
        total_ref[...] = before_ref[...]


def slope_kernel(
    group, own_ref, near_ref, *refs
):
    before_ref = None if group == 1 else refs[0]
    slope_ref, kind_ref, own_cols, diagonal, picked, listed, table = refs[-7:]
    signs = signs_of(group)

    @pl.when(pl.program_id(0) == 0)
    def _():
        spread_own(own_ref, own_cols)
        picked[...] = jnp.zeros_like(picked)
        start_from(before_ref, kind_ref)

    mark_diagonal(group, diagonal)
    mark_listed(own_ref, near_ref, signs, picked, listed)
    one_hots = [kind_rows(near_ref, near) for near in range(COLUMN)]
    fill_table(table, one_hots, near_ref, signs)
    for block in range(COLUMN):
        for near in range(COLUMN):
            rows = near_rows(listed, near_ref, signs, block, near)
            for start in range(0, SLOTS, CHUNK):
                left = left_over(rows, own_cols, diagonal, block, near, start)
                middle = left - 0.5
                square = middle * middle
                cosine = middle * horner(ODD, square)
                sine = horner(EVEN, square)
                twice = cosine + cosine
                last = -2.0 * left
                last_g = (left * left) * (sine * (-2.0 * math.pi))
                now = last * cosine + 0.5 * last_g
                now_g = last_g * cosine
                span = (pl.ds(block * SLOTS + start, CHUNK), pl.ds(near * SLOTS, SLOTS))
                slope_ref[0, 0, span[0], span[1]] = last.astype(BF16)
                slope_ref[0, 1, span[0], span[1]] = now.astype(BF16)
                for order in range(2, ORDERS):
                    last, now = now, twice * now - last + now_g
                    if order < ORDERS - 1:
                        last_g, now_g = now_g, twice * now_g - last_g
                    slope_ref[0, order, span[0], span[1]] = now.astype(BF16)
    sums = dot(slope_ref[0].reshape(ORDERS * ATOMS, ATOMS), table[...], ((1,), (1,)))
    kind_ref[...] += sums.reshape(ORDERS, ATOMS, SLOTS)


def true_rows(near_ref, signs, near):
    steps = steps_to(near_ref, near, signs)
    x = (near_ref[0, near, 0:1, :] + SIDE * steps[0]) * (1.0 / REACH)
    y = (near_ref[0, near, 1:2, :] + SIDE * steps[1]) * (1.0 / REACH)
    return x, y, near_ref[0, near, 2:3, :] * (1.0 / REACH)


def kind_rows(near_ref, near):
    kinds = lax.broadcasted_iota(jnp.int32, (KINDS, SLOTS), 0).astype(F32)
    return jnp.where(near_ref[0, near, 3:4, :] == kinds, 1.0, 0.0)


def fill_table(table, values, near_ref, signs):
    for near in range(COLUMN):
        zero = jnp.zeros((KINDS, SLOTS), F32)
        pieces = [values[near] if part == near else zero for part in range(COLUMN)]
        for row in true_rows(near_ref, signs, near):
            product = values[near] * row
            high = product.astype(BF16).astype(F32)
            pieces.extend((high, product - high))
        pieces.extend([zero] * (SLOTS // KINDS - PARTS))
        table[:, pl.ds(near * SLOTS, SLOTS)] = jnp.concatenate(pieces, axis=0).astype(BF16)


def pair_kernel(
    group, own_ref, near_ref, slope_ref, near_hidden_ref, near_grad_ref, hidden_ref, grad_ref,
    radial_ref, *refs,
):
    before_ref = None if group == 1 else refs[0]
    force_ref, own_cols, left_side, right_side = refs[-4:]
    signs = signs_of(group)

    @pl.when(pl.program_id(0) == 0)
    def _():
        spread_own(own_ref, own_cols)
        start_from(before_ref, force_ref)
        for block in range(COLUMN):
            span = pl.ds(block * SLOTS, SLOTS)
            grad = grad_ref[0, span, :].astype(F32)
            hidden = hidden_ref[0, span, :].astype(F32)
            for order in range(ORDERS):
                radial = radial_ref[order : order + 1, :]
                place = pl.ds(order * SLOTS, SLOTS)
                left_side[block, place, 0:CHANNELS] = (radial * grad).astype(BF16)
                left_side[block, place, CHANNELS : 2 * CHANNELS] = (radial * hidden).astype(BF16)

    right_side[:, 0:CHANNELS] = near_hidden_ref[0]
    right_side[:, CHANNELS : 2 * CHANNELS] = near_grad_ref[0]
    near_places = [true_rows(near_ref, signs, near) for near in range(COLUMN)]
    for block in range(COLUMN):
        pair = dot(left_side[block], right_side[...], ((1,), (1,)))
        for start in range(0, SLOTS, CHUNK):
            span = pl.ds(block * SLOTS + start, CHUNK)
            strength = jnp.zeros((CHUNK, ATOMS), F32)
            for order in range(ORDERS):
                rows = pair[order * SLOTS + start : order * SLOTS + start + CHUNK, :]
                strength = strength + rows * slope_ref[0, order, span, :].astype(F32)
            for axis in range(3):
                total = force_ref[axis, span, :]
                for near in range(COLUMN):
                    row = near_places[near][axis]
                    if axis == 2:
                        row = row + (SIDE / REACH) * offset_z(block, near)
                    part = strength[:, near * SLOTS : (near + 1) * SLOTS]
                    total = total + part * (row - own_cols[axis, span, :])
                force_ref[axis, span, :] = total


def kind_kernel(group, slope_ref, projected_ref, near_ref, *refs):
    before_ref = None if group == 1 else refs[0]
    near_kind_ref, table = refs[-2:]

    @pl.when(pl.program_id(0) == 0)
    def _():
        start_from(before_ref, near_kind_ref)

    add_kinds(signs_of(group), slope_ref, projected_ref, near_ref, near_kind_ref, table)


def add_kinds(signs, slope_ref, projected_ref, near_ref, near_kind, table):
    projected = projected_ref[0].astype(F32)
    total = near_kind[...]
    for order in range(ORDERS):
        values = [
            projected[order * KINDS : (order + 1) * KINDS, near * SLOTS : (near + 1) * SLOTS]
            for near in range(COLUMN)
        ]
        fill_table(table.at[order], values, near_ref, signs)
        total = total + dot(slope_ref[0, order], table[order], ((1,), (1,)))
    near_kind[...] = total


def last_kernel(
    slope_ref, projected_ref, near_ref, before_ref, own_projected_ref, own_ref, force_ref,
    kind_ref, mixed_ref, mass_ref, new_force_ref, new_velocity_ref, own_cols, table, near_kind,
):
    @pl.when(pl.program_id(0) == 0)
    def _():
        spread_own(own_ref, own_cols)
        near_kind[...] = before_ref[...]

    add_kinds(signs_of(2), slope_ref, projected_ref, near_ref, near_kind, table)

    @pl.when(pl.program_id(0) == 2)
    def _():
        lanes = lax.broadcasted_iota(jnp.int32, (SLOTS, SLOTS), 1)
        lane_kind = (lanes % KINDS).astype(F32)
        part = lanes // KINDS
        inner = lax.broadcasted_iota(jnp.int32, (ORDERS * KINDS, SLOTS), 0)
        outer = lax.broadcasted_iota(jnp.int32, (ORDERS * KINDS, SLOTS), 1) % KINDS
        slots = lax.broadcasted_iota(jnp.int32, (1, SLOTS), 1)
        for block in range(COLUMN):
            span = pl.ds(block * SLOTS, SLOTS)
            kinds = turned(own_ref[0, block, 3:4, :])
            total = jnp.where(kinds == lane_kind, near_kind[span, :], 0.0)
            own = own_projected_ref[0, :, span]
            for order in range(ORDERS):
                chosen = jnp.where(inner == outer + order * KINDS, 1.0, 0.0).astype(BF16)
                spread = dot(own, chosen, ((0,), (0,)))
                total = total + spread * kind_ref[order, span, :]
            for axis in range(3):
                factor = jnp.zeros((SLOTS, SLOTS), F32)
                for near in range(COLUMN):
                    shift = -own_cols[axis, span, :]
                    if axis == 2:
                        shift = shift + (SIDE / REACH) * offset_z(block, near)
                    factor = jnp.where(part == near, shift, factor)
                here = jnp.logical_or(
                    part == COLUMN + 2 * axis, part == COLUMN + 1 + 2 * axis
                )
                factor = jnp.where(here, 1.0, factor)
                lanes_force = force_ref[axis, span, :] + total * factor
                summed = jnp.sum(lanes_force.T, axis=0, keepdims=True)
                live = slots.astype(F32) < own_ref[0, block, 4:5, :]
                force = jnp.where(live, summed * (2.0 / REACH), 0.0)
                row = 3 * block + axis
                new_force_ref[row] = force
                new_velocity_ref[row] = mixed_ref[row] + HALF_STEP * force / mass_ref[block]


RADIAL_ONE = 0
RADIAL_TWO = ORDERS
TABLE = ORDERS * KINDS
MIX_ONE = CHANNELS
MIX_TWO = 2 * CHANNELS
WIDE = 3 * CHANNELS
UPSTREAM = 2 * ATOMS
WEIGHT_ROWS = 3 * ATOMS


def prepare_kernel(
    parity_ref, counts_ref, masses_ref, positions_ref, velocities_ref, forces_ref, noise_ref, species_ref,
    pair_list_ref, embedding_ref, radial_one_ref, radial_two_ref, mix_one_ref, mix_two_ref,
    readout_ref, new_positions_ref, geometry_ref, mixed_ref, mass_ref, weights_ref,
):
    geometry_ref[...] = jnp.zeros_like(geometry_ref)
    kinds = embedding_ref.shape[0]
    weights_ref[RADIAL_ONE : RADIAL_ONE + ORDERS, :] = radial_one_ref[...]
    weights_ref[RADIAL_TWO : RADIAL_TWO + ORDERS, :] = radial_two_ref[...].astype(F32)
    weights_ref[MIX_ONE : MIX_ONE + CHANNELS, :] = mix_one_ref[...].astype(F32)
    weights_ref[MIX_TWO : MIX_TWO + CHANNELS, :] = mix_two_ref[...].astype(F32)
    weights_ref[WIDE : WIDE + SLOTS, :] = jnp.zeros((SLOTS, CHANNELS), F32)
    weights_ref[WIDE : WIDE + kinds, :] = embedding_ref[...].astype(F32)
    for order in range(ORDERS):
        weights_ref[TABLE + order * KINDS : TABLE + (order + 1) * KINDS, :] = (
            radial_one_ref[order : order + 1, :] * weights_ref[WIDE : WIDE + KINDS, :]
        )
    slots = lax.broadcasted_iota(jnp.int32, (SLOTS, CHANNELS), 0)
    for block in range(COLUMN):
        live = slots < counts_ref[0, 0, block]
        start = UPSTREAM + block * SLOTS
        weights_ref[start : start + SLOTS, :] = jnp.where(live, readout_ref[...], 0.0)
        species = species_ref[block]
        mass = jnp.zeros((1, SLOTS), F32)
        for kind in range(kinds):
            mass = jnp.where(species == kind, masses_ref[kind], mass)
        mass_ref[block] = mass
        for axis in range(3):
            row = 3 * block + axis
            half_velocity = velocities_ref[row] + HALF_STEP * forces_ref[row] / mass
            half_position = positions_ref[row] + HALF_STEP * half_velocity
            mixed = (
                DECAY * half_velocity
                + jnp.sqrt((1.0 - DECAY * DECAY) / mass) * noise_ref[row]
            )
            new_positions = half_position + HALF_STEP * mixed
            mixed_ref[row] = mixed
            new_positions_ref[row] = new_positions
            geometry_ref[block, axis : axis + 1, :] = new_positions
        geometry_ref[block, 3:4, :] = species.astype(F32)
        geometry_ref[block, 4:5, :] = jnp.full(
            (1, SLOTS), counts_ref[0, 0, block], jnp.int32
        ).astype(F32)
        for axis in range(2):
            geometry_ref[block, 6 + axis : 7 + axis, :] = jnp.full(
                (1, SLOTS), 1 - 2 * parity_ref[axis], jnp.int32
            ).astype(F32)
        geometry_ref[block, 5:6, 0:13] = pair_list_ref[block].astype(F32)


def swap(cell, axis, first):
    count = lax.axis_size(axis)
    pairs = [((first + i) % count, (first + i + 1) % count) for i in range(0, count, 2)]
    return lax.ppermute(cell, axis, pairs + [(right, left) for left, right in pairs])


def own_row(cell):
    return jnp.stack([swap(cell, "gx", 0), cell, swap(cell, "gx", 1)])


def outer_rows(row):
    return swap(row, "gy", 0), swap(row, "gy", 1)


SMEM = pl.BlockSpec(memory_space=pltpu.SMEM)


def whole(*shape):
    return pl.BlockSpec(
        shape, lambda column: (0,) * len(shape), pipeline_mode=pl.Buffered(1)
    )


def weight(first, rows):
    return pl.BlockSpec(
        (rows, CHANNELS), lambda column: (first // rows, 0), pipeline_mode=pl.Buffered(1)
    )


def result(*shape):
    return pl.BlockSpec(shape, lambda column: (0,) * len(shape))


def at_column(*shape):
    return pl.BlockSpec((1,) + shape, lambda column: (column,) + (0,) * len(shape))


def at_centre(*shape):
    return pl.BlockSpec((1,) + shape, lambda column: (1,) + (0,) * len(shape))


def outer_specs(*shape):
    zeros = (0,) * len(shape)
    return [
        pl.BlockSpec((1,) + shape, lambda column: (jnp.minimum(column, 2),) + zeros),
        pl.BlockSpec((1,) + shape, lambda column: (jnp.maximum(column - 3, 0),) + zeros),
    ]


def call(kernel, name, columns, out_shape, in_specs, out_specs, scratch, flops):
    return pl.pallas_call(
        kernel,
        name=name,
        out_shape=out_shape,
        grid=(columns,),
        in_specs=in_specs,
        out_specs=out_specs,
        scratch_shapes=scratch,
        cost_estimate=pl.CostEstimate(
            flops=columns * flops, bytes_accessed=columns * PAIR_BYTES, transcendentals=0
        ),
        compiler_params=pltpu.CompilerParams(
            dimension_semantics=("arbitrary",), vmem_limit_bytes=LIMIT
        ),
    )


def shape_of(*shape, kind=F32):
    return jax.ShapeDtypeStruct(shape, kind)


PAIR_BYTES = ORDERS * ATOMS * ATOMS * 2
PAIR_FLOPS = ORDERS * ATOMS * ATOMS * CHANNELS * 2


def on_device(
    positions, velocities, forces, noise, species, counts, pair_list, masses, embedding,
    radial_one, mix_one, radial_two, mix_two, readout,
):
    vmem = pl.BlockSpec(memory_space=pltpu.VMEM)
    rows = (3 * COLUMN, 1, SLOTS)
    parity = jnp.stack([lax.axis_index("gx") % 2, lax.axis_index("gy") % 2])
    new_positions, geometry, mixed_velocity, atom_mass, weights = pl.pallas_call(
        prepare_kernel,
        name="prepare",
        out_shape=(
            shape_of(*rows),
            shape_of(COLUMN, 8, SLOTS),
            shape_of(*rows),
            shape_of(COLUMN, 1, SLOTS),
            shape_of(WEIGHT_ROWS, CHANNELS),
        ),
        in_specs=[SMEM] * 3 + [vmem] * 12,
    )(
        parity, counts, masses, positions.reshape(rows), velocities.reshape(rows), forces.reshape(rows),
        noise.reshape(rows), species.reshape(COLUMN, 1, SLOTS), pair_list.reshape(COLUMN, 1, 13),
        embedding, radial_one, radial_two, mix_one, mix_two, readout[None, :],
    )

    cols = pltpu.VMEM((3, ATOMS, SLOTS), F32)
    place = pltpu.VMEM((1, COLUMN, 8, SLOTS), F32)
    message = pltpu.VMEM((ATOMS, CHANNELS), F32)
    square = pltpu.VMEM((SLOTS, SLOTS), F32)
    flags = [pltpu.VMEM((16, SLOTS), F32), pltpu.VMEM((16, SLOTS), F32)]
    pairs = (ORDERS, ATOMS, ATOMS)
    cell = (COLUMN, 8, SLOTS)
    field = (ATOMS, CHANNELS)
    own_spec = at_centre(*cell)
    radial_one_spec = weight(RADIAL_ONE, ORDERS)
    radial_two_spec = weight(RADIAL_TWO, ORDERS)
    mix_one_spec = weight(MIX_ONE, CHANNELS)
    mix_two_spec = weight(MIX_TWO, CHANNELS)
    wide_spec = weight(WIDE, SLOTS)
    upstream_spec = weight(UPSTREAM, ATOMS)

    geometry_row = own_row(geometry)
    geometry_outer = outer_rows(geometry_row)
    geometries = (geometry_outer[0], geometry_row, geometry_outer[1])
    basis_scratch = [cols, place, square, *flags, message, pltpu.VMEM(field, BF16)]
    basis_row, message_row = call(
        functools.partial(basis_kernel, 1),
        "basis_row",
        3,
        (shape_of(3, *pairs, kind=BF16), shape_of(*field)),
        [own_spec, at_column(*cell), wide_spec, radial_one_spec],
        (at_column(*pairs), result(*field)),
        basis_scratch,
        PAIR_FLOPS,
    )(geometry_row, geometry_row, weights, weights)
    basis_outer, hidden, first_gate = call(
        functools.partial(basis_kernel, OUTER),
        "basis_outer",
        6,
        (shape_of(6, *pairs, kind=BF16), shape_of(*field, kind=BF16), shape_of(*field)),
        [own_spec, *outer_specs(*cell), wide_spec, radial_one_spec, mix_one_spec, whole(*field)],
        (at_column(*pairs), result(*field), result(*field)),
        basis_scratch,
        PAIR_FLOPS,
    )(geometry_row, *geometry_outer, weights, weights, weights, message_row)

    def slope_of(group, before):
        sums = (ORDERS, ATOMS, SLOTS)
        return call(
            functools.partial(slope_kernel, group),
            f"slope_{group}",
            3,
            (shape_of(3, *pairs, kind=BF16), shape_of(*sums)),
            [own_spec, at_column(*cell)] + [whole(*sums)] * len(before),
            (at_column(*pairs), result(*sums)),
            [cols, square, *flags, pltpu.VMEM((SLOTS, ATOMS), BF16)],
            PAIR_FLOPS,
        )(geometry_row, geometries[group], *before)

    def single(kernel, name, out_shape, scratch, *operands):
        return pl.pallas_call(
            kernel,
            name=name,
            out_shape=out_shape,
            in_specs=[vmem] * len(operands),
            out_specs=vmem,
            scratch_shapes=scratch,
            cost_estimate=pl.CostEstimate(
                flops=6 * PAIR_FLOPS, bytes_accessed=6 * PAIR_BYTES, transcendentals=0
            ),
            compiler_params=pltpu.CompilerParams(vmem_limit_bytes=LIMIT),
        )(*operands)

    def gather_row(name, row):
        return single(gather_kernel, name, shape_of(*field), [], basis_row, row, weights)

    hidden_row = own_row(hidden)
    slope_1, kind_sums = slope_of(1, ())
    hidden_row, kind_sums = lax.optimization_barrier((hidden_row, kind_sums))
    hidden_outer = outer_rows(hidden_row)
    second_row = gather_row("second_row", hidden_row)
    slope_0, kind_sums = slope_of(0, (kind_sums,))
    second_row, kind_sums = lax.optimization_barrier((second_row, kind_sums))
    message_grad = single(
        second_kernel, "second_outer", shape_of(*field, kind=BF16), [message],
        basis_outer, *hidden_outer, weights, second_row,
    )

    grad_row = own_row(message_grad)
    slope_2, kind_sums = slope_of(2, (kind_sums,))
    grad_row, kind_sums = lax.optimization_barrier((grad_row, kind_sums))
    slopes = (slope_0, slope_1, slope_2)
    grad_outer = outer_rows(grad_row)
    projected = single(
        first_kernel, "first_outer", shape_of(ORDERS * KINDS, ATOMS, kind=BF16), [message],
        basis_outer, *grad_outer, weights, first_gate, gather_row("first_row", grad_row),
    )

    hiddens = (hidden_outer[0], hidden_row, hidden_outer[1])
    grads = (grad_outer[0], grad_row, grad_outer[1])
    forces_so_far = ()
    for group in (1, 0, 2):
        total = call(
            functools.partial(pair_kernel, group),
            f"pair_{group}",
            3,
            shape_of(3, ATOMS, SLOTS),
            [
                own_spec, at_column(*cell), at_column(*pairs), at_column(*field),
                at_column(*field), at_centre(*field), at_centre(*field), radial_two_spec,
            ]
            + [whole(3, ATOMS, SLOTS)] * len(forces_so_far),
            result(3, ATOMS, SLOTS),
            [
                cols, pltpu.VMEM((COLUMN, ORDERS * SLOTS, 2 * CHANNELS), BF16),
                pltpu.VMEM((ATOMS, 2 * CHANNELS), BF16),
            ],
            2 * PAIR_FLOPS,
        )(
            geometry_row, geometries[group], slopes[group], hiddens[group], grads[group],
            hidden_row, grad_row, weights, *forces_so_far,
        )
        forces_so_far = (total,)

    projected_row = own_row(projected)
    projected_outer = outer_rows(projected_row)
    projecteds = (projected_outer[0], projected_row, projected_outer[1])
    kinds = (ORDERS * KINDS, ATOMS)
    tables = pltpu.VMEM((ORDERS, SLOTS, ATOMS), BF16)
    kind_specs = [at_column(*pairs), at_column(*kinds), at_column(*cell)]
    near_kind = ()
    for group in (1, 0):
        near_kind = (
            call(
                functools.partial(kind_kernel, group),
                f"last_{group}",
                3,
                shape_of(ATOMS, SLOTS),
                kind_specs + [whole(ATOMS, SLOTS)] * len(near_kind),
                result(ATOMS, SLOTS),
                [tables],
                PAIR_FLOPS,
            )(slopes[group], projecteds[group], geometries[group], *near_kind),
        )
    new_forces, new_velocities = call(
        last_kernel,
        "last_2",
        3,
        (shape_of(*rows), shape_of(*rows)),
        kind_specs
        + [
            whole(ATOMS, SLOTS), at_centre(*kinds), own_spec, whole(3, ATOMS, SLOTS),
            whole(ORDERS, ATOMS, SLOTS), whole(*rows), whole(COLUMN, 1, SLOTS),
        ],
        (result(*rows), result(*rows)),
        [cols, tables, pltpu.VMEM((ATOMS, SLOTS), F32)],
        PAIR_FLOPS,
    )(
        slopes[2], projecteds[2], geometries[2], *near_kind, projected_row, geometry_row,
        *forces_so_far, kind_sums, mixed_velocity, atom_mass,
    )
    return tuple(
        value.reshape(positions.shape) for value in (new_positions, new_velocities, new_forces)
    )


def solution(mesh):
    split_spec = P("gx", "gy")
    return jax.shard_map(
        on_device,
        mesh=mesh,
        in_specs=(split_spec,) * 7 + (P(),) * 7,
        out_specs=(split_spec,) * 3,
        check_vma=False,
    )
```
